256 devices in a mesh: dp: 4 (over y_hi, core), bank: 64 (over y_lo, x, z).
Axes of the slice: x: 4, y: 4 (y_hi: 2, y_lo: 2; y = y_hi * 2 + y_lo), z: 8, core: 2. Of those that a mesh axis runs over, the one named last changes fastest.
Arguments:
- features: bfloat16 [64, 4096, 256], P('dp', 'bank'), may hold values from -6 to 6
- patch_index: int32 [64, 128], P('dp'), may hold values from 0 to 4095, as said below
- positive_index: int32 [8192], P('dp'), may hold values from 0 to 262143
- bank: bfloat16 [262144, 256], P('bank'), may hold values from -0.4 to 0.4
Outputs:
- loss: float32 [8192], P(('dp', 'bank'))
- query_grad: float32 [8192, 256], P(('dp', 'bank'))
- mean_loss: float32 [], replicated
The draws below stay inside these ranges and needn't reach their ends.
Inputs may be any that keep to these rules, and one draw needn't show every extreme that they name: `patch_index`: within one image the sampled positions are distinct.
All inputs are finite; a program needn't handle non-finite values.
Results may differ from the reference program's by a relative error of at most 0.00065.
Values may be sent and summed in bfloat16 or wider, within the bound.
A program may use at most 64 MiB of HBM per device.

```python
import math
import jax
import jax.numpy as jnp
from jax import lax

C = 256
PATCHES = 128
IMAGES = 64
QUERIES = 8192
HW = 4096
NB = 262144
N_BANK = 64


def draw_patch_index(key, part):
    keys = jax.random.split(jax.random.fold_in(key, 11), IMAGES)
    chosen = jax.vmap(lambda single: jax.random.permutation(single, HW)[:PATCHES])(keys)
    return chosen.astype(jnp.int32)


def draw_bank(key, part):
    key_noise, key_common, key_gain = jax.random.split(jax.random.fold_in(key, 23), 3)
    noise = jax.random.uniform(key_noise, (NB, C), jnp.float32, -1.0, 1.0)
    common = jax.random.uniform(key_common, (1, C), jnp.float32, -1.0, 1.0)
    position = jnp.arange(NB, dtype=jnp.float32)[:, None] / NB
    mixing = 0.3
    gain = jax.random.uniform(key_gain, (NB, 1), jnp.float32, 0.8, 1.2)
    scale = (1.0 + position) * gain * (math.sqrt(3.0) / 16.0)
    return (scale * (noise + mixing * common)).astype(jnp.bfloat16)


def touch_ends(drawn, key, least, top_value):
    longest = drawn.shape.index(max(drawn.shape))
    spots = []
    for shift in (0, 1):
        where = [jax.random.randint(jax.random.fold_in(key, axis), (), 0, length) for axis, length in enumerate(drawn.shape)]
        where[longest] = (where[longest] + shift) % drawn.shape[longest]
        spots.append(tuple(where))
    return drawn.at[spots[0]].set(least).at[spots[1]].set(top_value)


def block_scale(own_key, dims, cuts, low, high):
    def one(dim, shards_of):
        steps = jax.random.uniform(jax.random.fold_in(jax.random.fold_in(own_key, 6), dim), (shards_of,), jnp.float32, low / len(cuts), high / len(cuts))
        return jnp.repeat(jnp.exp(steps), dims[dim] // shards_of).reshape((-1,) + (1,) * (len(dims) - dim - 1))

    factor_of = one(*cuts[0])
    for cut in cuts[1:]:
        factor_of = factor_of * one(*cut)
    return factor_of


def bell_draw(rng, shape, spread, most, cuts=(), held_as=jnp.bfloat16):
    factor_of = block_scale(rng, shape, cuts, -0.22, 0.18) if cuts else 1.0
    drawn = jax.random.normal(rng, shape, jnp.float32) * spread * factor_of
    return jnp.minimum(jnp.maximum(drawn, -most), most).astype(held_as)


def setup_inputs(seed: int = 0) -> dict:
    streams_of = jax.random.split(jax.random.key(seed), 5)
    features = bell_draw(streams_of[0], (IMAGES, HW, C), 1.0, 6.0, ((0, 4), (1, 64)))
    patch_index = draw_patch_index(jax.random.fold_in(streams_of[4], 71), 0)
    positive_index = touch_ends(jax.random.randint(streams_of[2], (QUERIES,), 0, NB), jax.random.fold_in(streams_of[2], 1), 0, NB - 1).astype(jnp.int32)
    bank = draw_bank(jax.random.fold_in(streams_of[4], 71), 0)
    return {"features": features, "patch_index": patch_index, "positive_index": positive_index, "bank": bank}


SOFTMAX_TEMP = 0.07
EPSILON = 1e-05

def normalize(values):
    scale = lax.rsqrt(lax.optimization_barrier(jnp.mean(values * values, axis=-1, keepdims=True)) + EPSILON)
    return values * scale / math.sqrt(values.shape[-1])

def reference(features, patch_index, positive_index, bank):
    picked = jnp.take_along_axis(features, patch_index[:, :, None], axis=1)
    raw = picked.reshape(-1, picked.shape[-1]).astype(jnp.float32)
    query_vector = normalize(raw).astype(jnp.bfloat16)
    shards = bank.reshape(N_BANK, -1, bank.shape[-1])

    def visit(carry, bank_block):
        exponent_sum, weighted_negatives = carry
        logit_scores = jnp.dot(query_vector, bank_block.T, preferred_element_type=jnp.float32) / SOFTMAX_TEMP
        exponent_terms = jnp.exp(logit_scores - 1.0 / SOFTMAX_TEMP)
        exponent_sum = exponent_sum + lax.optimization_barrier(jnp.sum(exponent_terms, axis=1))
        weighted_negatives = weighted_negatives + jnp.dot(exponent_terms.astype(jnp.bfloat16), bank_block, preferred_element_type=jnp.float32)
        return ((exponent_sum, weighted_negatives), None)
    start = (jnp.zeros((raw.shape[0],), jnp.float32), jnp.zeros(raw.shape, jnp.float32))
    (exponent_sum, weighted_negatives), _ = lax.scan(visit, start, shards)
    positive_key = bank[positive_index].astype(jnp.float32)
    matched_logit = lax.optimization_barrier(jnp.sum(query_vector.astype(jnp.float32) * positive_key, axis=1)) / SOFTMAX_TEMP
    loss = jnp.log(exponent_sum) + 1.0 / SOFTMAX_TEMP - matched_logit
    query_update = (weighted_negatives / exponent_sum[:, None] - positive_key) / SOFTMAX_TEMP
    _, pullback = jax.vjp(normalize, raw)
    query_grad = pullback(query_update)[0]
    return (loss, query_grad, jnp.mean(loss))
```

```python
import itertools
import math

import jax
import jax.numpy as jnp
from jax import lax
from jax.experimental import pallas as pl
from jax.experimental.pallas import tpu as pltpu
from jax.sharding import PartitionSpec as P

SOFTMAX_TEMP = 0.07
EPSILON = 1e-05
MESH = pl.DeviceIdType.MESH
F32, BF16 = jnp.float32, jnp.bfloat16

NY, NX, NZ = 2, 4, 8
ROWS = 32
HALF = NZ * ROWS
N_SEMS = 96


def bank_id(y, x, z):
    return (y * NX + x) * NZ + z


def kernel(
    count_all,
    patch_ref,
    pos_ref,
    feat_ref,
    bank_ref,
    loss_ref,
    grad_ref,
    mean_ref,
    fb, fa, fu, fm, fc, fs, fz, fy,
    pb, pa, pu, pm, pc, ps, pz, py,
    qa, raw,
    wf, wb, wa, wu, wm, wc, ws, wo, wz, wys, wy,
    acc, tacc,
    ts, tx, t2, tz, t3, ty, tt,
    ms, mx, mz, my,
    col,
    ssem, rsem,
):
    place, dp = lax.axis_index("bank"), lax.axis_index("dp")
    y, x, z = place // (NX * NZ), (place // NZ) % NX, place % NZ
    corner = (dp // 2) * 4 + y * 2 + dp % 2
    xp, xo, xm = (x + 1) % NX, (x + 2) % NX, (x + 3) % NX
    x_peers = [{"bank": bank_id(y, (x + k) % NX, z)} for k in range(1, NX)]
    z_at = [(z + k) % NZ for k in range(1, NZ)]
    z_peers = [{"bank": bank_id(y, x, at)} for at in z_at]
    y_peer = {"bank": bank_id(1 - y, x, z)}
    c_peers = []
    for k in range(1, 8):
        other = (corner + k) % 8
        c_peers.append(
            {"dp": (other // 4) * 2 + other % 2, "bank": bank_id((other // 2) % 2, x, z)}
        )
    plus, minus = x_peers[0], x_peers[2]
    count = itertools.count()

    def remote(src, dst, peer):
        i = next(count)
        return pltpu.make_async_remote_copy(
            src_ref=src,
            dst_ref=dst,
            send_sem=ssem.at[i],
            recv_sem=rsem.at[i],
            device_id=peer,
            device_id_type=MESH,
        )

    started = []

    def go(copies):
        for copy in copies:
            copy.start()
            started.append(copy)

    barrier = pltpu.get_barrier_semaphore()
    greeted = x_peers + z_peers + c_peers
    for peer in greeted:
        pl.semaphore_signal(barrier, inc=1, device_id=peer, device_id_type=MESH)

    images, spots, channels = feat_ref.shape
    patches = patch_ref.shape[0]
    for i in range(images):
        hit = patch_ref[:, i : i + 1] == lax.broadcasted_iota(jnp.int32, (patches, spots), 1)
        picked = jnp.dot(hit.astype(BF16), feat_ref[i], preferred_element_type=F32)
        first = i * patches
        fb[first // HALF % NX, first // (HALF * NX), pl.ds(first % HALF, patches), :] = (
            picked.astype(BF16)
        )
    pl.semaphore_wait(barrier, len(greeted))

    def x_first(b, a, u):
        return [
            remote(b.at[xo, 0], a.at[0], plus),
            remote(b.at[xo, 1], a.at[1], minus),
            remote(b.at[xp, 1], u.at[1], plus),
            remote(b.at[xm, 0], u.at[0], minus),
        ]

    def x_second(m, c):
        return [remote(m.at[0], c.at[0], plus), remote(m.at[1], c.at[1], minus)]

    def z_send(s, r):
        return [
            remote(s.at[:, at], r.at[k], peer) for k, (at, peer) in enumerate(zip(z_at, z_peers))
        ]

    def merge_exact(b, a, m, first, second):
        first[0].wait_recv()
        m[0] = a[0] + b[xp, 0]
        go(second[:1])
        first[1].wait_recv()
        m[1] = a[1] + b[xm, 1]
        go(second[1:])

    def x_total_exact(b, u, c, s, first, second):
        first[2].wait_recv()
        first[3].wait_recv()
        second[0].wait_recv()
        second[1].wait_recv()
        for h in range(NY):
            s[h] = (b[x, h] + u[h] + c[h]).reshape(NZ, ROWS, channels)

    def z_total_exact(s, r, copies):
        total = s[:, z]
        for k, copy in enumerate(copies):
            copy.wait_recv()
            total = total + r[k]
        return total

    f1, f2 = x_first(fb, fa, fu), x_second(fm, fc)
    go(f1)

    bank_dev = bank_ref.shape[0]
    for g in range(pos_ref.shape[1]):
        col[pl.ds(g * 128, 128), :] = pos_ref[:, g : g + 1]
    wide = 1024

    def take(block, carry):
        rows = col[pl.ds(pl.multiple_of(block * HALF, HALF), HALF), :]

        def part(j, _):
            start = pl.multiple_of(j * wide, wide)
            keys = lax.broadcasted_iota(jnp.int32, (HALF, wide), 1) + start
            one = jnp.where(rows == keys, 1.0, 0.0).astype(BF16)
            got = jnp.dot(one, bank_ref[pl.ds(start, wide), :], preferred_element_type=F32)
            acc[...] = acc[...] + got
            return 0

        acc[...] = jnp.zeros_like(acc)
        lax.fori_loop(0, bank_dev // wide, part, 0)
        pb[block % NX, block // NX] = acc[...].astype(BF16)
        return carry

    lax.fori_loop(0, NX * NY, take, 0)

    merge_exact(fb, fa, fm, f1, f2)
    x_total_exact(fb, fu, fc, fs, f1, f2)
    f3 = z_send(fs, fz)
    go(f3)
    p1, p2 = x_first(pb, pa, pu), x_second(pm, pc)
    go(p1)
    fs[:, z] = z_total_exact(fs, fz, f3)
    f4 = remote(fs.at[1 - y, z], fy, y_peer)
    go([f4])
    f4.wait_recv()
    own = (fs[y, z] + fy[...]).astype(F32)
    raw[...] = own
    scale = lax.rsqrt(jnp.mean(own * own, axis=-1, keepdims=True) + EPSILON)
    qa[x, y, z] = (own * scale / math.sqrt(channels)).astype(BF16)

    g1 = remote(qa.at[x, y, z], qa.at[x, y, z], y_peer)
    go([g1])
    merge_exact(pb, pa, pm, p1, p2)
    g1.wait_recv()
    g2 = [remote(qa.at[x, :, z], qa.at[x, :, z], peer) for peer in z_peers]
    go(g2)
    x_total_exact(pb, pu, pc, ps, p1, p2)
    for copy in g2:
        copy.wait_recv()
    g3 = [
        remote(qa.at[x, 0], qa.at[x, 0], plus),
        remote(qa.at[x, 1], qa.at[x, 1], minus),
        remote(qa.at[x, 1], qa.at[x, 1], plus),
        remote(qa.at[x, 0], qa.at[x, 0], minus),
    ]
    g4 = [
        remote(qa.at[xm, 0], qa.at[xm, 0], plus),
        remote(qa.at[xp, 1], qa.at[xp, 1], minus),
    ]
    go(g3)
    p3 = z_send(ps, pz)
    go(p3)

    factor = 1.0 / (SOFTMAX_TEMP * math.log(2.0))
    block_keys = 2048

    def unit(at, h):
        query = qa[at, h].reshape(HALF, channels)
        acc[...] = jnp.zeros_like(acc)
        tacc[...] = jnp.zeros_like(tacc)

        def step(j, _):
            keys = bank_ref[pl.ds(pl.multiple_of(j * block_keys, block_keys), block_keys), :]
            dots = lax.dot_general(
                query, keys, (((1,), (1,)), ((), ())), preferred_element_type=F32
            )
            terms = jnp.exp2(dots * factor - factor)
            some = terms[:, :128]
            for lane in range(128, block_keys, 128):
                some = some + terms[:, lane : lane + 128]
            tacc[...] = tacc[...] + some
            acc[...] = acc[...] + jnp.dot(terms.astype(BF16), keys, preferred_element_type=F32)
            return 0

        lax.fori_loop(0, bank_dev // block_keys, step, 0)
        sums = jnp.sum(jnp.transpose(tacc[...]), axis=0, keepdims=True)
        ts[at, pl.ds(2 * h, 1), :] = sums[:, :128]
        ts[at, pl.ds(2 * h + 1, 1), :] = sums[:, 128:]

    ts[...] = jnp.zeros_like(ts)
    unit(x, 0)
    wf[0] = acc[...]
    g3[0].wait_recv()
    g3[1].wait_recv()
    go(g4)
    unit(x, 1)
    wf[1] = acc[...]
    w1, w2 = x_first(wb, wa, wu), x_second(wm, wc)

    g3[3].wait_recv()
    unit(xp, 0)
    wf[2] = acc[...]
    unit(xp, 1)
    wb[xp, 1] = acc[...].astype(BF16)
    go(w1[2:3])
    g4[0].wait_recv()
    g4[1].wait_recv()
    unit(xo, 0)
    wb[xo, 0] = acc[...].astype(BF16)
    go(w1[0:1])
    unit(xo, 1)
    wb[xo, 1] = acc[...].astype(BF16)
    go(w1[1:2])
    g3[2].wait_recv()
    unit(xm, 0)
    wb[xm, 0] = acc[...].astype(BF16)
    go(w1[3:4])
    w1[0].wait_recv()
    wm[0] = (wa[0].astype(F32) + wf[2]).astype(BF16)
    go(w2[:1])
    unit(xm, 1)
    t1 = [remote(ts.at[(x + k) % NX], tx.at[k - 1], x_peers[k - 1]) for k in range(1, NX)]
    go(t1)
    w1[1].wait_recv()
    wm[1] = (wa[1].astype(F32) + acc[...]).astype(BF16)
    go(w2[1:])

    ps[:, z] = z_total_exact(ps, pz, p3)
    p4 = remote(ps.at[1 - y, z], py, y_peer)
    go([p4])

    total = ts[x]
    for k, copy in enumerate(t1):
        copy.wait_recv()
        total = total + tx[k]
    t2[...] = total
    t4 = [remote(t2, tz.at[k], peer) for k, peer in enumerate(z_peers)]
    go(t4)

    w1[2].wait_recv()
    w1[3].wait_recv()
    w2[0].wait_recv()
    w2[1].wait_recv()
    for h in range(NY):
        part = wf[h] + wu[h].astype(F32) + wc[h].astype(F32)
        part = part.reshape(NZ, ROWS, channels)
        wo[h] = part
        ws[h] = part.astype(BF16)
    w3 = z_send(ws, wz)
    go(w3)

    total = t2[...]
    for k, copy in enumerate(t4):
        copy.wait_recv()
        total = total + tz[k]
    t3[...] = total
    t5 = remote(t3, ty, y_peer)
    go([t5])
    p4.wait_recv()
    positive = (ps[y, z] + py[...]).astype(F32)
    query = qa[x, y, z].astype(F32)
    matched = jnp.sum(query * positive, axis=1, keepdims=True) / SOFTMAX_TEMP
    t5.wait_recv()
    tt[...] = t3[...] + ty[...]
    line = tt[pl.ds(2 * y + z // 4, 1), :]
    lane = lax.broadcasted_iota(jnp.int32, (ROWS, 128), 1)
    row = lax.broadcasted_iota(jnp.int32, (ROWS, 128), 0)
    mine = jnp.where(lane == row + (z % 4) * ROWS, jnp.broadcast_to(line, (ROWS, 128)), 0.0)
    exponent_sum = jnp.sum(mine, axis=1, keepdims=True)
    loss = jnp.log(exponent_sum) + 1.0 / SOFTMAX_TEMP - matched
    diagonal = lax.broadcasted_iota(jnp.int32, (ROWS, ROWS), 0) == lax.broadcasted_iota(
        jnp.int32, (ROWS, ROWS), 1
    )
    loss_ref[...] = jnp.sum(
        jnp.where(diagonal, jnp.broadcast_to(loss, (ROWS, ROWS)), 0.0), axis=0, keepdims=True
    )

    ms[0] = jnp.broadcast_to(jnp.sum(loss, axis=0, keepdims=True), (8, 128))
    m1 = [remote(ms.at[0], mx.at[k], peer) for k, peer in enumerate(x_peers)]
    go(m1)
    for k, copy in enumerate(m1):
        copy.wait_recv()
    ms[1] = ms[0] + (mx[0] + mx[1] + mx[2])
    m2 = [remote(ms.at[1], mz.at[k], peer) for k, peer in enumerate(z_peers)]
    go(m2)

    part = wo[:, z]
    for k, copy in enumerate(w3):
        copy.wait_recv()
        part = part + wz[k].astype(F32)
    wys[...] = part
    w4 = remote(wys.at[1 - y], wy, y_peer)
    go([w4])

    losses = ms[1]
    for k, copy in enumerate(m2):
        copy.wait_recv()
        losses = losses + mz[k]
    ms[2] = losses
    m3 = [remote(ms.at[2], my.at[k], peer) for k, peer in enumerate(c_peers)]
    go(m3)

    w4.wait_recv()
    weighted = wys[y] + wy[...]
    step = (weighted / exponent_sum - positive) / SOFTMAX_TEMP
    own = raw[...]
    scale = lax.rsqrt(jnp.mean(own * own, axis=-1, keepdims=True) + EPSILON)
    inner = jnp.mean(step * own, axis=-1, keepdims=True)
    grad_ref[...] = (scale / math.sqrt(channels)) * (step - own * (scale * scale * inner))

    losses = ms[2]
    for k, copy in enumerate(m3):
        copy.wait_recv()
        losses = losses + my[k]
    mean_ref[...] = losses[:1] / count_all
    for copy in started:
        copy.wait_send()


def on_device(features, patch_index, positive_index, bank):
    place = lax.axis_index("bank")
    images, hw_dev, channels = features.shape
    patches = patch_index.shape[1]
    queries_dp = images * patches
    spots = jnp.transpose(patch_index) - place * hw_dev
    keys = jnp.transpose(positive_index.reshape(-1, 128)) - place * bank.shape[0]
    count_all = queries_dp * lax.axis_size("dp")

    def vmem(dtype, *shape):
        return pltpu.VMEM(shape, dtype)

    def exact():
        return [
            vmem(BF16, NX, NY, HALF, channels),
            *[vmem(BF16, NY, HALF, channels) for _ in range(4)],
            vmem(BF16, NY, NZ, ROWS, channels),
            vmem(BF16, NZ - 1, NY, ROWS, channels),
            vmem(BF16, ROWS, channels),
        ]

    scratch = [
        *exact(),
        *exact(),
        vmem(BF16, NX, NY, NZ, ROWS, channels),
        vmem(F32, ROWS, channels),
        vmem(F32, 3, HALF, channels),
        vmem(BF16, NX, NY, HALF, channels),
        *[vmem(BF16, NY, HALF, channels) for _ in range(4)],
        vmem(BF16, NY, NZ, ROWS, channels),
        vmem(F32, NY, NZ, ROWS, channels),
        vmem(BF16, NZ - 1, NY, ROWS, channels),
        vmem(F32, NY, ROWS, channels),
        vmem(F32, ROWS, channels),
        vmem(F32, HALF, channels),
        vmem(F32, HALF, 128),
        vmem(F32, NX, 8, 128),
        vmem(F32, NX - 1, 8, 128),
        vmem(F32, 8, 128),
        vmem(F32, NZ - 1, 8, 128),
        vmem(F32, 8, 128),
        vmem(F32, 8, 128),
        vmem(F32, 8, 128),
        vmem(F32, 3, 8, 128),
        vmem(F32, 3, 8, 128),
        vmem(F32, 7, 8, 128),
        vmem(F32, 7, 8, 128),
        vmem(jnp.int32, queries_dp, 1),
        pltpu.SemaphoreType.DMA((N_SEMS,)),
        pltpu.SemaphoreType.DMA((N_SEMS,)),
    ]
    loss, grad, mean = pl.pallas_call(
        lambda *refs: kernel(count_all, *refs),
        out_shape=(
            jax.ShapeDtypeStruct((1, ROWS), F32),
            jax.ShapeDtypeStruct((ROWS, channels), F32),
            jax.ShapeDtypeStruct((1, 128), F32),
        ),
        in_specs=[pl.BlockSpec(memory_space=pltpu.VMEM)] * 4,
        out_specs=[pl.BlockSpec(memory_space=pltpu.VMEM)] * 3,
        scratch_shapes=scratch,
        compiler_params=pltpu.CompilerParams(
            collective_id=0, has_side_effects=True, vmem_limit_bytes=56 << 20
        ),
        name="patch_nce",
    )(spots, keys, features, bank)
    return (loss.reshape(ROWS), grad, mean[0, 0])


def solution(mesh):
    in_specs = (P("dp", "bank", None), P("dp", None), P("dp"), P("bank", None))
    out_specs = (P(("dp", "bank")), P(("dp", "bank"), None), P())
    return jax.shard_map(
        on_device, mesh=mesh, in_specs=in_specs, out_specs=out_specs, check_vma=False
    )
```

```python
import itertools
import math

import jax
import jax.numpy as jnp
from jax import lax
from jax.experimental import pallas as pl
from jax.experimental.pallas import tpu as pltpu
from jax.sharding import PartitionSpec as P

SOFTMAX_TEMP = 0.07
EPSILON = 1e-05
MESH = pl.DeviceIdType.MESH
F32, BF16 = jnp.float32, jnp.bfloat16

NY, NX, NZ, ND = 2, 4, 8, 4
NG = NY * NZ
ROWS = 32
CHUNKS = 2
PART = ROWS // CHUNKS
HALF = NZ * PART
N_SEMS = 208


def bank_id(y, x, z):
    return (y * NX + x) * NZ + z


def kernel(
    count_all,
    patch_ref,
    pos_ref,
    feat_hbm,
    bank_hbm,
    loss_ref,
    grad_ref,
    mean_ref,
    feat_ref, bank_ref,
    fb, fa, fu, fm, fc, fs, fz,
    pb, pa, pu, pm, pc, ps, pz,
    qa, raw,
    wf, wb, wa, wu, wm, wc, ws, wo, wz,
    acc, tacc,
    ts, tx, tg, ms,
    col,
    ssem, rsem, lsem,
):
    load_feat = pltpu.make_async_copy(feat_hbm, feat_ref, lsem.at[0])
    load_bank = pltpu.make_async_copy(bank_hbm, bank_ref, lsem.at[1])
    load_feat.start()
    load_bank.start()
    place, dp = lax.axis_index("bank"), lax.axis_index("dp")
    y, x, z = place // (NX * NZ), (place // NZ) % NX, place % NZ
    xp, xo, xm = (x + 1) % NX, (x + 2) % NX, (x + 3) % NX
    x_peers = [{"bank": bank_id(y, (x + k) % NX, z)} for k in range(1, NX)]
    plus, minus = x_peers[0], x_peers[2]
    here = y * NZ + z
    g_at = [((here + k) % NG // NZ, (here + k) % NZ) for k in range(1, NG)]
    g_peers = [{"bank": bank_id(gy, x, gz)} for gy, gz in g_at]
    spot = x * ND + dp
    m_peers = []
    for k in range(1, NX * ND):
        other = (spot + k) % (NX * ND)
        m_peers.append({"dp": other % ND, "bank": bank_id(y, other // ND, z)})
    count = itertools.count()

    def remote(src, dst, peer):
        i = next(count)
        return pltpu.make_async_remote_copy(
            src_ref=src,
            dst_ref=dst,
            send_sem=ssem.at[i],
            recv_sem=rsem.at[i],
            device_id=peer,
            device_id_type=MESH,
        )

    started = []

    def go(*copies):
        for copy in copies:
            copy.start()
            started.append(copy)

    def arrived(*copies):
        for copy in copies:
            copy.wait_recv()

    barrier = pltpu.get_barrier_semaphore()
    greeted = g_peers + m_peers
    for peer in greeted:
        pl.semaphore_signal(barrier, inc=1, device_id=peer, device_id_type=MESH)

    images, spots, channels = feat_ref.shape
    patches = patch_ref.shape[1]
    spread = jnp.transpose(patch_ref[...] - place * spots)
    load_feat.wait()
    for i in range(images):
        hit = spread[:, i : i + 1] == lax.broadcasted_iota(jnp.int32, (patches, spots), 1)
        picked = jnp.dot(hit.astype(BF16), feat_ref[i], preferred_element_type=F32).astype(BF16)
        picked = picked.reshape(patches // ROWS, CHUNKS, PART, channels)
        first = i * patches
        at = first // (NZ * ROWS)
        row = first % (NZ * ROWS) // CHUNKS
        for c in range(CHUNKS):
            fb[c, at % NX, at // NX, pl.ds(row, patches // CHUNKS), :] = picked[:, c].reshape(
                patches // CHUNKS, channels
            )
    pl.semaphore_wait(barrier, len(greeted))

    def over_x(b, a, u, m, c):
        return (
            [remote(b.at[xo, 0], a.at[0], plus), remote(b.at[xo, 1], a.at[1], minus)],
            [remote(b.at[xp, 1], u.at[1], plus), remote(b.at[xm, 0], u.at[0], minus)],
            [remote(m.at[0], c.at[0], plus), remote(m.at[1], c.at[1], minus)],
        )

    def merge(b, a, m, copies):
        arrived(copies[0][0])
        m[0] = a[0] + b[xp, 0]
        go(copies[2][0])
        arrived(copies[0][1])
        m[1] = a[1] + b[xm, 1]
        go(copies[2][1])

    def x_total(b, u, c, s, copies):
        arrived(*copies[1], *copies[2])
        for h in range(NY):
            s[h] = (b[x, h] + u[h] + c[h]).reshape(s.shape[1:])

    def over_group(s, r):
        return [
            remote(s.at[gy, gz], r.at[k], peer)
            for k, ((gy, gz), peer) in enumerate(zip(g_at, g_peers))
        ]

    def g_total(s, r, copies):
        total = s[y, z]
        for k, copy in enumerate(copies):
            arrived(copy)
            total = total + r[k]
        return total

    bank_dev = bank_ref.shape[0]
    wide = 2048

    def take(low, high):
        def block(at, carry):
            rows = col[pl.ds(pl.multiple_of(at * NZ * ROWS, NZ * ROWS), NZ * ROWS), :]
            acc[...] = jnp.zeros_like(acc)

            def some(j, _):
                start = pl.multiple_of(j * wide, wide)
                keys = lax.broadcasted_iota(jnp.int32, (NZ * ROWS, wide), 1) + start
                one = jnp.where(rows == keys, 1.0, 0.0).astype(BF16)
                acc[...] = acc[...] + jnp.dot(
                    one, bank_ref[pl.ds(start, wide), :], preferred_element_type=F32
                )
                return 0

            lax.fori_loop(0, bank_dev // wide, some, 0)
            pb[at % NX, at // NX] = acc[...].astype(BF16)
            return carry

        lax.fori_loop(low, high, block, 0)

    f = [over_x(fb.at[c], fa.at[c], fu.at[c], fm.at[c], fc.at[c]) for c in range(CHUNKS)]
    fg = [over_group(fs.at[c], fz.at[c]) for c in range(CHUNKS)]
    go(*f[0][0], *f[0][1], *f[1][0])
    spread = jnp.transpose(pos_ref[...] - place * bank_dev)
    for g in range(pos_ref.shape[0]):
        col[pl.ds(g * 128, 128), :] = spread[:, g : g + 1]
    load_bank.wait()
    take(0, 2)
    merge(fb.at[0], fa.at[0], fm.at[0], f[0])
    go(*f[1][1])
    take(2, 3)
    merge(fb.at[1], fa.at[1], fm.at[1], f[1])
    take(3, 5)
    x_total(fb.at[0], fu.at[0], fc.at[0], fs.at[0], f[0])
    go(*fg[0])
    take(5, 6)
    x_total(fb.at[1], fu.at[1], fc.at[1], fs.at[1], f[1])
    go(*fg[1])
    take(6, 8)
    p = over_x(pb, pa, pu, pm, pc)
    pg = over_group(ps, pz)
    go(*p[0], *p[1])

    def unit_rows(own):
        scale = lax.rsqrt(jnp.mean(own * own, axis=-1, keepdims=True) + EPSILON)
        return own * scale / math.sqrt(channels)

    qg = []
    for c in range(CHUNKS):
        own = g_total(fs.at[c], fz.at[c], fg[c]).astype(F32)
        raw[pl.ds(c * PART, PART), :] = own
        qa[c, x, y, z] = unit_rows(own).astype(BF16)
        mine = qa.at[c, x, y, z]
        qg.append([remote(mine, mine, peer) for peer in g_peers])
        go(*qg[c])
    merge(pb, pa, pm, p)

    def spread_x(c):
        return (
            [remote(qa.at[c, x, 0], qa.at[c, x, 0], plus), remote(qa.at[c, x, 1], qa.at[c, x, 1], minus)],
            [remote(qa.at[c, x, 1], qa.at[c, x, 1], plus), remote(qa.at[c, x, 0], qa.at[c, x, 0], minus)],
            [remote(qa.at[c, xm, 0], qa.at[c, xm, 0], plus), remote(qa.at[c, xp, 1], qa.at[c, xp, 1], minus)],
        )

    qx = [spread_x(c) for c in range(CHUNKS)]
    factor = 1.0 / (SOFTMAX_TEMP * math.log(2.0))
    block_keys = 2048

    def unit(c, at):
        query = qa[c, at].reshape(NY * HALF, channels)
        acc[...] = jnp.zeros_like(acc)
        tacc[...] = jnp.zeros_like(tacc)

        def step(j, _):
            keys = bank_ref[pl.ds(pl.multiple_of(j * block_keys, block_keys), block_keys), :]
            dots = lax.dot_general(
                query, keys, (((1,), (1,)), ((), ())), preferred_element_type=F32
            )
            terms = jnp.exp2(dots * factor - factor)
            some = terms[:, :128]
            for lane in range(128, block_keys, 128):
                some = some + terms[:, lane : lane + 128]
            tacc[...] = tacc[...] + some
            acc[...] = acc[...] + jnp.dot(terms.astype(BF16), keys, preferred_element_type=F32)
            return 0

        lax.fori_loop(0, bank_dev // block_keys, step, 0)
        sums = jnp.sum(jnp.transpose(tacc[...]), axis=0, keepdims=True)
        for h in range(NY):
            ts[at, pl.ds(NY * c + h, 1), :] = sums[:, h * HALF : (h + 1) * HALF]

    ts[...] = jnp.zeros_like(ts)
    arrived(*qg[0])
    go(*qx[0][0], *qx[0][1])
    unit(0, x)
    wo[0] = acc[...].reshape(wo.shape[1:])
    arrived(*qx[0][0])
    go(*qx[0][2])
    arrived(*qg[1])
    go(*qx[1][0], *qx[1][1])
    x_total(pb, pu, pc, ps, p)
    go(*pg)
    arrived(*qx[0][1])
    w = [over_x(wb.at[c], wa.at[c], wu.at[c], wm.at[c], wc.at[c]) for c in range(CHUNKS)]
    wg = [over_group(ws.at[c], wz.at[c]) for c in range(CHUNKS)]

    def push_plus(c):
        unit(c, xp)
        wf[c] = acc[pl.ds(0, HALF), :]
        wb[c, xp, 1] = acc[pl.ds(HALF, HALF), :].astype(BF16)
        go(w[c][1][0])

    def push_across(c):
        unit(c, xo)
        wb[c, xo, 0] = acc[pl.ds(0, HALF), :].astype(BF16)
        wb[c, xo, 1] = acc[pl.ds(HALF, HALF), :].astype(BF16)
        go(*w[c][0])

    def push_minus(c):
        unit(c, xm)
        wb[c, xm, 0] = acc[pl.ds(0, HALF), :].astype(BF16)
        go(w[c][1][1])
        arrived(*w[c][0])
        wm[c, 0] = (wa[c, 0].astype(F32) + wf[c]).astype(BF16)
        go(w[c][2][0])
        wm[c, 1] = (wa[c, 1].astype(F32) + acc[pl.ds(HALF, HALF), :]).astype(BF16)
        go(w[c][2][1])

    def push_total(c):
        arrived(*w[c][1], *w[c][2])
        for h in range(NY):
            part = wu[c, h].astype(F32) + wc[c, h].astype(F32)
            part = wo[c, h] + part.reshape(NZ, PART, channels)
            wo[c, h] = part
            ws[c, h] = part.astype(BF16)
        go(*wg[c])

    push_plus(0)
    arrived(*qx[1][0])
    go(*qx[1][2])
    arrived(*qx[0][2])
    push_across(0)
    push_minus(0)
    arrived(*qx[1][1], *qx[1][2])
    push_across(1)
    push_plus(1)
    positive = g_total(ps, pz, pg).astype(F32)
    query = qa[:, x, y, z].reshape(ROWS, channels).astype(F32)
    matched = jnp.sum(query * positive, axis=1, keepdims=True) / SOFTMAX_TEMP
    push_total(0)
    push_minus(1)
    t1 = [remote(ts.at[(x + k) % NX], tx.at[k - 1], x_peers[k - 1]) for k in range(1, NX)]
    go(*t1)
    unit(1, x)
    wo[1] = acc[...].reshape(wo.shape[1:])

    total = ts[x]
    for k, copy in enumerate(t1):
        arrived(copy)
        total = total + tx[k]
    line = lax.broadcasted_iota(jnp.int32, (8, 128), 0)
    tg[here] = jnp.where(
        line == 4, jnp.broadcast_to(jnp.sum(matched, axis=0, keepdims=True), (8, 128)), total
    )
    t2 = [remote(tg.at[here], tg.at[here], peer) for peer in g_peers]
    go(*t2)
    push_total(1)
    arrived(*t2)
    total = tg[0]
    for k in range(1, NG):
        total = total + tg[k]
    lane = lax.broadcasted_iota(jnp.int32, (PART, HALF), 1)
    row = lax.broadcasted_iota(jnp.int32, (PART, HALF), 0)
    parts = []
    for c in range(CHUNKS):
        sums = jnp.where(y == 0, total[NY * c : NY * c + 1], total[NY * c + 1 : NY * c + 2])
        mine = jnp.where(lane == row + z * PART, jnp.broadcast_to(sums, (PART, HALF)), 0.0)
        parts.append(jnp.sum(mine, axis=1, keepdims=True))
    exponent_sum = jnp.concatenate(parts, axis=0)
    logs = jnp.sum(jnp.log(total[: NY * CHUNKS]), axis=0, keepdims=True)
    logs = jnp.sum(logs, axis=1, keepdims=True)
    quarter = logs + NG * ROWS / SOFTMAX_TEMP - total[4:5, :1]
    ms[spot] = jnp.broadcast_to(quarter, (8, 128))
    m1 = [remote(ms.at[spot], ms.at[spot], peer) for peer in m_peers]
    go(*m1)

    loss = jnp.log(exponent_sum) + 1.0 / SOFTMAX_TEMP - matched
    diagonal = lax.broadcasted_iota(jnp.int32, (ROWS, ROWS), 0) == lax.broadcasted_iota(
        jnp.int32, (ROWS, ROWS), 1
    )
    loss_ref[...] = jnp.sum(
        jnp.where(diagonal, jnp.broadcast_to(loss, (ROWS, ROWS)), 0.0), axis=0, keepdims=True
    )
    own = raw[...]
    scale = lax.rsqrt(jnp.mean(own * own, axis=-1, keepdims=True) + EPSILON)
    for c in range(CHUNKS):
        weighted = wo[c, y, z]
        for k, copy in enumerate(wg[c]):
            arrived(copy)
            weighted = weighted + wz[c, k].astype(F32)
        some = slice(c * PART, (c + 1) * PART)
        step = (weighted / exponent_sum[some] - positive[some]) / SOFTMAX_TEMP
        inner = jnp.mean(step * own[some], axis=-1, keepdims=True)
        s = scale[some]
        grad_ref[pl.ds(c * PART, PART), :] = (s / math.sqrt(channels)) * (
            step - own[some] * (s * s * inner)
        )
    arrived(*m1)
    losses = ms[0]
    for k in range(1, NX * ND):
        losses = losses + ms[k]
    mean_ref[...] = losses[:1] / count_all
    for copy in started:
        copy.wait_send()


def on_device(features, patch_index, positive_index, bank):
    images, hw_dev, channels = features.shape
    queries_dp = images * patch_index.shape[1]
    count_all = queries_dp * lax.axis_size("dp")

    def vmem(dtype, *shape):
        return pltpu.VMEM(shape, dtype)

    def chunked(*lead, rows):
        return [
            vmem(BF16, *lead, NX, NY, NZ * rows, channels),
            *[vmem(BF16, *lead, NY, NZ * rows, channels) for _ in range(4)],
            vmem(BF16, *lead, NY, NZ, rows, channels),
            vmem(BF16, *lead, NG - 1, rows, channels),
        ]

    scratch = [
        vmem(BF16, *features.shape),
        vmem(BF16, *bank.shape),
        *chunked(CHUNKS, rows=PART),
        *chunked(rows=ROWS),
        vmem(BF16, CHUNKS, NX, NY, NZ, PART, channels),
        vmem(F32, ROWS, channels),
        vmem(F32, CHUNKS, HALF, channels),
        *chunked(CHUNKS, rows=PART)[:6],
        vmem(F32, CHUNKS, NY, NZ, PART, channels),
        vmem(BF16, CHUNKS, NG - 1, PART, channels),
        vmem(F32, NY * HALF, channels),
        vmem(F32, NY * HALF, 128),
        vmem(F32, NX, 8, 128),
        vmem(F32, NX - 1, 8, 128),
        vmem(F32, NG, 8, 128),
        vmem(F32, NX * ND, 8, 128),
        vmem(jnp.int32, queries_dp, 1),
        pltpu.SemaphoreType.DMA((N_SEMS,)),
        pltpu.SemaphoreType.DMA((N_SEMS,)),
        pltpu.SemaphoreType.DMA((2,)),
    ]
    near, far = pl.BlockSpec(memory_space=pltpu.VMEM), pl.BlockSpec(memory_space=pl.ANY)
    loss, grad, mean = pl.pallas_call(
        lambda *refs: kernel(count_all, *refs),
        out_shape=(
            jax.ShapeDtypeStruct((1, ROWS), F32),
            jax.ShapeDtypeStruct((ROWS, channels), F32),
            jax.ShapeDtypeStruct((1, 128), F32),
        ),
        in_specs=[near, near, far, far],
        out_specs=[near] * 3,
        scratch_shapes=scratch,
        compiler_params=pltpu.CompilerParams(
            collective_id=0, has_side_effects=True, vmem_limit_bytes=56 << 20
        ),
        name="patch_nce",
    )(patch_index, positive_index.reshape(-1, 128), features, bank)
    return (loss.reshape(ROWS), grad, mean[0, 0])


def solution(mesh):
    in_specs = (P("dp", "bank", None), P("dp", None), P("dp"), P("bank", None))
    out_specs = (P(("dp", "bank")), P(("dp", "bank"), None), P())
    return jax.shard_map(
        on_device, mesh=mesh, in_specs=in_specs, out_specs=out_specs, check_vma=False
    )
```

```python
import itertools
import math

import jax
import jax.numpy as jnp
from jax import lax
from jax.experimental import pallas as pl
from jax.experimental.pallas import tpu as pltpu
from jax.sharding import PartitionSpec as P

SOFTMAX_TEMP = 0.07
EPSILON = 1e-05
MESH = pl.DeviceIdType.MESH
F32, BF16 = jnp.float32, jnp.bfloat16

NY, NX, NZ, ND = 2, 4, 8, 4
NG = NY * NZ
ROWS = 32
CHUNKS = 2
PART = ROWS // CHUNKS
HALF = NZ * PART
N_SEMS = 48


def bank_id(y, x, z):
    return (y * NX + x) * NZ + z


def kernel(
    count_all,
    patch_hbm,
    pos_hbm,
    feat_hbm,
    bank_hbm,
    loss_ref,
    grad_ref,
    mean_ref,
    patch_ref, pos_ref, feat_ref, bank_ref,
    fb, fa, fu, fm, fc, fs, fz,
    pb, pa, pu, pm, pc, ps, pz,
    qa, raw,
    wf, wb, wa, wu, wm, wc, ws, wo, wz,
    acc, tacc,
    ts, tx, tg, ms,
    col,
    sems, lsem,
):
    loads = [
        pltpu.make_async_copy(far, near, lsem.at[i])
        for i, (far, near) in enumerate(
            [(patch_hbm, patch_ref), (feat_hbm, feat_ref), (pos_hbm, pos_ref), (bank_hbm, bank_ref)]
        )
    ]
    for load in loads:
        load.start()
    place, dp = lax.axis_index("bank"), lax.axis_index("dp")
    y, x, z = place // (NX * NZ), (place // NZ) % NX, place % NZ
    xp, xo, xm = (x + 1) % NX, (x + 2) % NX, (x + 3) % NX
    x_peers = [{"bank": bank_id(y, (x + k) % NX, z)} for k in range(1, NX)]
    plus, minus = x_peers[0], x_peers[2]
    here = y * NZ + z
    g_at = [((here + k) % NG // NZ, (here + k) % NZ) for k in range(1, NG)]
    g_peers = [{"bank": bank_id(gy, x, gz)} for gy, gz in g_at]
    spot = x * ND + dp
    m_peers = []
    for k in range(1, NX * ND):
        other = (spot + k) % (NX * ND)
        m_peers.append({"dp": other % ND, "bank": bank_id(y, other // ND, z)})
    count = itertools.count()
    sent = []

    def channel():
        return sems.at[next(count)]

    def remote(src, dst, peer, out, into):
        return pltpu.make_async_remote_copy(
            src_ref=src,
            dst_ref=dst,
            send_sem=out,
            recv_sem=into,
            device_id=peer,
            device_id_type=MESH,
        )

    def take_all(sized, sem):
        pltpu.make_async_copy(sized, sized, sem).wait()

    def go(*copies):
        for copy in copies:
            copy.start()

    barrier = pltpu.get_barrier_semaphore()
    greeted = g_peers + m_peers
    for peer in greeted:
        pl.semaphore_signal(barrier, inc=1, device_id=peer, device_id_type=MESH)

    images, spots, channels = feat_ref.shape
    patches = patch_ref.shape[1]
    loads[0].wait()
    columns = jnp.transpose(patch_ref[...] - place * spots)
    loads[1].wait()
    for i in range(images):
        hit = columns[:, i : i + 1] == lax.broadcasted_iota(jnp.int32, (patches, spots), 1)
        picked = jnp.dot(hit.astype(BF16), feat_ref[i], preferred_element_type=F32).astype(BF16)
        picked = picked.reshape(patches // ROWS, CHUNKS, PART, channels)
        first = i * patches
        at = first // (NZ * ROWS)
        row = first % (NZ * ROWS) // CHUNKS
        for c in range(CHUNKS):
            fb[c, at % NX, at // NX, pl.ds(row, patches // CHUNKS), :] = picked[:, c].reshape(
                patches // CHUNKS, channels
            )
    pl.semaphore_wait(barrier, len(greeted))

    def over_x(b, a, u, m, c):
        out, across, last = channel(), channel(), channel()
        sent.append((b.at[pl.ds(0, 3)], out))
        return (
            [
                remote(b.at[xo, 0], a.at[0], plus, out, across),
                remote(b.at[xo, 1], a.at[1], minus, out, across),
            ],
            [
                remote(b.at[xp, 1], u.at[1], plus, out, last),
                remote(b.at[xm, 0], u.at[0], minus, out, last),
            ],
            [
                remote(m.at[0], c.at[0], plus, out, last),
                remote(m.at[1], c.at[1], minus, out, last),
            ],
            (a, across),
            (b.at[pl.ds(0, 2)], last),
        )

    def merge(b, a, m, copies):
        take_all(*copies[3])
        m[0] = a[0] + b[xp, 0]
        m[1] = a[1] + b[xm, 1]
        go(*copies[2])

    def x_total(b, u, c, s, copies):
        take_all(*copies[4])
        for h in range(NY):
            s[h] = (b[x, h] + u[h] + c[h]).reshape(s.shape[1:])

    def over_group(s, r):
        out, into = channel(), channel()
        sent.append((r, out))
        copies = [
            remote(s.at[gy, gz], r.at[k], peer, out, into)
            for k, ((gy, gz), peer) in enumerate(zip(g_at, g_peers))
        ]
        return copies, (r, into)

    def g_total(s, r, stage):
        take_all(*stage[1])
        total = s[y, z]
        for k in range(NG - 1):
            total = total + r[k]
        return total

    bank_dev = bank_ref.shape[0]
    wide = 2048

    def take(at, h):
        first = pl.multiple_of((h * NX + at) * NZ * ROWS, NZ * ROWS)
        rows = col[pl.ds(first, NZ * ROWS), :]
        acc[...] = jnp.zeros_like(acc)

        def some(j, _):
            start = pl.multiple_of(j * wide, wide)
            keys = lax.broadcasted_iota(jnp.int32, (NZ * ROWS, wide), 1) + start
            one = jnp.where(rows == keys, 1.0, 0.0).astype(BF16)
            acc[...] = acc[...] + jnp.dot(
                one, bank_ref[pl.ds(start, wide), :], preferred_element_type=F32
            )
            return 0

        lax.fori_loop(0, bank_dev // wide, some, 0)
        pb[at, h] = acc[...].astype(BF16)

    f = [over_x(fb.at[c], fa.at[c], fu.at[c], fm.at[c], fc.at[c]) for c in range(CHUNKS)]
    fg = [over_group(fs.at[c], fz.at[c]) for c in range(CHUNKS)]
    go(*f[0][0], *f[0][1], *f[1][0])
    loads[2].wait()
    columns = jnp.transpose(pos_ref[...] - place * bank_dev)
    for g in range(pos_ref.shape[0]):
        col[pl.ds(g * 128, 128), :] = columns[:, g : g + 1]
    loads[3].wait()
    p = over_x(pb, pa, pu, pm, pc)
    pg = over_group(ps, pz)
    take(xo, 0)
    take(xo, 1)
    merge(fb.at[0], fa.at[0], fm.at[0], f[0])
    go(*f[1][1])
    take(xp, 1)
    merge(fb.at[1], fa.at[1], fm.at[1], f[1])
    take(xm, 0)
    x_total(fb.at[0], fu.at[0], fc.at[0], fs.at[0], f[0])
    go(*fg[0][0])
    go(*p[0], *p[1])
    take(xp, 0)
    take(xm, 1)
    x_total(fb.at[1], fu.at[1], fc.at[1], fs.at[1], f[1])
    go(*fg[1][0])
    take(x, 0)
    take(x, 1)
    merge(pb, pa, pm, p)

    def unit_rows(own):
        scale = lax.rsqrt(jnp.mean(own * own, axis=-1, keepdims=True) + EPSILON)
        return own * scale / math.sqrt(channels)

    near_peers = [{"bank": bank_id(y, x, (z + k) % NZ)} for k in range(1, NZ)]
    far_peers = [{"bank": bank_id(1 - y, x, (z + k) % NZ)} for k in range(NZ)]

    def spread(c):
        out, near, far, one, two, relayed = (channel() for _ in range(6))
        sent.append((fz.at[c], out))
        more = channel()
        sent.append((fb.at[c, pl.ds(0, 3)], more))
        own = qa.at[c, x, y, z]
        mine, other = qa.at[c, x, y], qa.at[c, x, 1 - y]

        def forward(h):
            source = qa.at[c, (x + 3 + 2 * h) % NX, h]
            target = {"bank": bank_id(y, (x + 1 + 2 * h) % NX, z)}
            return remote(source, source, target, more, relayed)

        return {
            "z": [remote(own, own, peer, out, near) for peer in near_peers]
            + [remote(own, own, peer, out, far) for peer in far_peers],
            "z_in": (fz.at[c, pl.ds(0, NZ - 1)], near),
            "y_in": (fz.at[c, pl.ds(0, NZ)], far),
            "one": [remote(mine, mine, peer, more, one) for peer in (plus, minus)],
            "one_in": (fb.at[c, 0], one),
            "two": [remote(other, other, peer, more, two) for peer in (plus, minus)],
            "two_in": (fb.at[c, 0], two),
            "first": [forward(y)],
            "second": [forward(1 - y)],
            "relay_in": (fb.at[c, 0], relayed),
        }

    q = [spread(c) for c in range(CHUNKS)]

    def query_rows(c):
        own = g_total(fs.at[c], fz.at[c], fg[c]).astype(F32)
        raw[pl.ds(c * PART, PART), :] = own
        qa[c, x, y, z] = unit_rows(own).astype(BF16)
        go(*q[c]["z"])

    query_rows(0)
    query_rows(1)

    factor = 1.0 / (SOFTMAX_TEMP * math.log(2.0))
    block_keys = 2048

    def unit(c, at):
        query = qa[c, at].reshape(NY * HALF, channels)
        acc[...] = jnp.zeros_like(acc)
        tacc[...] = jnp.zeros_like(tacc)

        def step(j, _):
            keys = bank_ref[pl.ds(pl.multiple_of(j * block_keys, block_keys), block_keys), :]
            dots = lax.dot_general(
                query, keys, (((1,), (1,)), ((), ())), preferred_element_type=F32
            )
            terms = jnp.exp2(dots * factor - factor)
            some = terms[:, :128]
            for lane in range(128, block_keys, 128):
                some = some + terms[:, lane : lane + 128]
            tacc[...] = tacc[...] + some
            acc[...] = acc[...] + jnp.dot(terms.astype(BF16), keys, preferred_element_type=F32)
            return 0

        lax.fori_loop(0, bank_dev // block_keys, step, 0)
        sums = jnp.sum(jnp.transpose(tacc[...]), axis=0, keepdims=True)
        for h in range(NY):
            ts[at, pl.ds(NY * c + h, 1), :] = sums[:, h * HALF : (h + 1) * HALF]

    ts[...] = jnp.zeros_like(ts)
    w = [over_x(wb.at[c], wa.at[c], wu.at[c], wm.at[c], wc.at[c]) for c in range(CHUNKS)]
    wg = [over_group(ws.at[c], wz.at[c]) for c in range(CHUNKS)]

    def push_own(c):
        unit(c, x)
        wo[c] = acc[...].reshape(wo.shape[1:])

    def push_plus(c):
        unit(c, xp)
        wf[c, 0] = acc[pl.ds(0, HALF), :]
        wb[c, xp, 1] = acc[pl.ds(HALF, HALF), :].astype(BF16)

    def push_minus(c):
        unit(c, xm)
        wf[c, 1] = acc[pl.ds(HALF, HALF), :]
        wb[c, xm, 0] = acc[pl.ds(0, HALF), :].astype(BF16)

    def push_across(c):
        unit(c, xo)
        wb[c, xo, 0] = acc[pl.ds(0, HALF), :].astype(BF16)
        wb[c, xo, 1] = acc[pl.ds(HALF, HALF), :].astype(BF16)

    def push_merged(c):
        take_all(*w[c][3])
        for h in range(NY):
            wm[c, h] = (wa[c, h].astype(F32) + wf[c, h]).astype(BF16)
        go(*w[c][2])

    def push_total(c):
        take_all(*w[c][4])
        for h in range(NY):
            part = wu[c, h].astype(F32) + wc[c, h].astype(F32)
            part = wo[c, h] + part.reshape(NZ, PART, channels)
            wo[c, h] = part
            ws[c, h] = part.astype(BF16)
        go(*wg[c][0])

    take_all(*q[0]["z_in"])
    go(*q[0]["one"])
    take_all(*q[0]["y_in"])
    go(*q[0]["two"])
    push_own(0)
    take_all(*q[0]["one_in"])
    go(*q[0]["first"])
    take_all(*q[1]["z_in"])
    go(*q[1]["one"])
    take_all(*q[0]["two_in"])
    go(*q[0]["second"])
    x_total(pb, pu, pc, ps, p)
    go(*pg[0])
    take_all(*q[1]["y_in"])
    go(*q[1]["two"])
    push_own(1)
    push_plus(0)
    take_all(*q[1]["one_in"])
    go(*q[1]["first"])
    go(w[0][1][0])
    take_all(*q[0]["relay_in"])
    push_across(0)
    take_all(*q[1]["two_in"])
    go(*q[1]["second"])
    go(*w[0][0])
    push_minus(0)
    go(w[0][1][1])
    take_all(*q[1]["relay_in"])
    push_across(1)
    go(*w[1][0])
    push_merged(0)
    push_plus(1)
    go(w[1][1][0])
    positive = g_total(ps, pz, pg).astype(F32)
    query = qa[:, x, y, z].reshape(ROWS, channels).astype(F32)
    matched = jnp.sum(query * positive, axis=1, keepdims=True) / SOFTMAX_TEMP
    push_minus(1)
    t1_out, t1_in = channel(), channel()
    sent.append((tx, t1_out))
    go(
        *[
            remote(ts.at[(x + k) % NX], tx.at[k - 1], x_peers[k - 1], t1_out, t1_in)
            for k in range(1, NX)
        ]
    )
    push_merged(1)
    go(w[1][1][1])

    take_all(tx, t1_in)
    total = ts[x]
    for k in range(NX - 1):
        total = total + tx[k]
    line = lax.broadcasted_iota(jnp.int32, (8, 128), 0)
    tg[here] = jnp.where(
        line == 4, jnp.broadcast_to(jnp.sum(matched, axis=0, keepdims=True), (8, 128)), total
    )
    t2_out, t2_in = channel(), channel()
    others = tg.at[pl.ds(0, NG - 1)]
    sent.append((others, t2_out))
    go(*[remote(tg.at[here], tg.at[here], peer, t2_out, t2_in) for peer in g_peers])
    push_total(0)
    push_total(1)
    take_all(others, t2_in)
    total = tg[0]
    for k in range(1, NG):
        total = total + tg[k]
    lane = lax.broadcasted_iota(jnp.int32, (PART, HALF), 1)
    row = lax.broadcasted_iota(jnp.int32, (PART, HALF), 0)
    parts = []
    for c in range(CHUNKS):
        sums = jnp.where(y == 0, total[NY * c : NY * c + 1], total[NY * c + 1 : NY * c + 2])
        mine = jnp.where(lane == row + z * PART, jnp.broadcast_to(sums, (PART, HALF)), 0.0)
        parts.append(jnp.sum(mine, axis=1, keepdims=True))
    exponent_sum = jnp.concatenate(parts, axis=0)
    logs = jnp.sum(jnp.log(total[: NY * CHUNKS]), axis=0, keepdims=True)
    logs = jnp.sum(logs, axis=1, keepdims=True)
    quarter = logs + NG * ROWS / SOFTMAX_TEMP - total[4:5, :1]
    ms[spot] = jnp.broadcast_to(quarter, (8, 128))
    m1_out, m1_in = channel(), channel()
    rest = ms.at[pl.ds(0, NX * ND - 1)]
    sent.append((rest, m1_out))
    go(*[remote(ms.at[spot], ms.at[spot], peer, m1_out, m1_in) for peer in m_peers])

    loss = jnp.log(exponent_sum) + 1.0 / SOFTMAX_TEMP - matched
    diagonal = lax.broadcasted_iota(jnp.int32, (ROWS, ROWS), 0) == lax.broadcasted_iota(
        jnp.int32, (ROWS, ROWS), 1
    )
    loss_ref[...] = jnp.sum(
        jnp.where(diagonal, jnp.broadcast_to(loss, (ROWS, ROWS)), 0.0), axis=0, keepdims=True
    )
    own = raw[...]
    scale = lax.rsqrt(jnp.mean(own * own, axis=-1, keepdims=True) + EPSILON)
    for c in range(CHUNKS):
        take_all(*wg[c][1])
        weighted = wo[c, y, z]
        for k in range(NG - 1):
            weighted = weighted + wz[c, k].astype(F32)
        some = slice(c * PART, (c + 1) * PART)
        step = (weighted / exponent_sum[some] - positive[some]) / SOFTMAX_TEMP
        inner = jnp.mean(step * own[some], axis=-1, keepdims=True)
        s = scale[some]
        grad_ref[pl.ds(c * PART, PART), :] = (s / math.sqrt(channels)) * (
            step - own[some] * (s * s * inner)
        )
    take_all(rest, m1_in)
    losses = ms[0]
    for k in range(1, NX * ND):
        losses = losses + ms[k]
    mean_ref[...] = losses[:1] / count_all
    for sized, sem in sent:
        take_all(sized, sem)


def on_device(features, patch_index, positive_index, bank):
    images, hw_dev, channels = features.shape
    queries_dp = images * patch_index.shape[1]
    count_all = queries_dp * lax.axis_size("dp")
    positions = positive_index.reshape(-1, 128)

    def vmem(dtype, *shape):
        return pltpu.VMEM(shape, dtype)

    def chunked(*lead, rows):
        return [
            vmem(BF16, *lead, NX, NY, NZ * rows, channels),
            *[vmem(BF16, *lead, NY, NZ * rows, channels) for _ in range(4)],
            vmem(BF16, *lead, NY, NZ, rows, channels),
            vmem(BF16, *lead, NG - 1, rows, channels),
        ]

    scratch = [
        vmem(jnp.int32, *patch_index.shape),
        vmem(jnp.int32, *positions.shape),
        vmem(BF16, *features.shape),
        vmem(BF16, *bank.shape),
        *chunked(CHUNKS, rows=PART),
        *chunked(rows=ROWS),
        vmem(BF16, CHUNKS, NX, NY, NZ, PART, channels),
        vmem(F32, ROWS, channels),
        vmem(F32, CHUNKS, NY, HALF, channels),
        *chunked(CHUNKS, rows=PART)[:6],
        vmem(F32, CHUNKS, NY, NZ, PART, channels),
        vmem(BF16, CHUNKS, NG - 1, PART, channels),
        vmem(F32, NY * HALF, channels),
        vmem(F32, NY * HALF, 128),
        vmem(F32, NX, 8, 128),
        vmem(F32, NX - 1, 8, 128),
        vmem(F32, NG, 8, 128),
        vmem(F32, NX * ND, 8, 128),
        vmem(jnp.int32, queries_dp, 1),
        pltpu.SemaphoreType.DMA((N_SEMS,)),
        pltpu.SemaphoreType.DMA((4,)),
    ]
    near, far = pl.BlockSpec(memory_space=pltpu.VMEM), pl.BlockSpec(memory_space=pl.ANY)
    loss, grad, mean = pl.pallas_call(
        lambda *refs: kernel(count_all, *refs),
        out_shape=(
            jax.ShapeDtypeStruct((1, ROWS), F32),
            jax.ShapeDtypeStruct((ROWS, channels), F32),
            jax.ShapeDtypeStruct((1, 128), F32),
        ),
        in_specs=[far] * 4,
        out_specs=[near] * 3,
        scratch_shapes=scratch,
        compiler_params=pltpu.CompilerParams(
            collective_id=0, has_side_effects=True, vmem_limit_bytes=56 << 20
        ),
        name="patch_nce",
    )(patch_index, positions, features, bank)
    return (loss.reshape(ROWS), grad, mean[0, 0])


def solution(mesh):
    in_specs = (P("dp", "bank", None), P("dp", None), P("dp"), P("bank", None))
    out_specs = (P(("dp", "bank")), P(("dp", "bank"), None), P())
    return jax.shard_map(
        on_device, mesh=mesh, in_specs=in_specs, out_specs=out_specs, check_vma=False
    )
```

```python
import itertools
import math

import jax
import jax.numpy as jnp
from jax import lax
from jax.experimental import pallas as pl
from jax.experimental.pallas import tpu as pltpu
from jax.sharding import PartitionSpec as P

SOFTMAX_TEMP = 0.07
EPSILON = 1e-05
MESH = pl.DeviceIdType.MESH
F32, BF16 = jnp.float32, jnp.bfloat16

NY, NX, NZ, ND = 2, 4, 8, 4
NG = NY * NZ
ROWS = 32
CHUNKS = 2
PART = ROWS // CHUNKS
HALF = NZ * PART
N_SEMS = 48


def bank_id(y, x, z):
    return (y * NX + x) * NZ + z


def kernel(
    count_all,
    patch_hbm,
    pos_hbm,
    feat_hbm,
    bank_hbm,
    loss_ref,
    grad_ref,
    mean_ref,
    patch_ref, pos_ref, feat_ref, bank_ref,
    fb, fa, fu, fm, fc, fs, fz,
    pb, pa, pu, pm, pc, ps, pz,
    qa, raw,
    wf, wb, wa, wu, wm, wc, ws, wo, wz,
    acc, tacc, held,
    ts, tx, tg, ms,
    col,
    sems, lsem,
):
    loads = [
        pltpu.make_async_copy(far, near, lsem.at[i])
        for i, (far, near) in enumerate(
            [(patch_hbm, patch_ref), (feat_hbm, feat_ref), (pos_hbm, pos_ref), (bank_hbm, bank_ref)]
        )
    ]
    for load in loads:
        load.start()
    place, dp = lax.axis_index("bank"), lax.axis_index("dp")
    y, x, z = place // (NX * NZ), (place // NZ) % NX, place % NZ
    xp, xo, xm = (x + 1) % NX, (x + 2) % NX, (x + 3) % NX
    x_peers = [{"bank": bank_id(y, (x + k) % NX, z)} for k in range(1, NX)]
    plus, minus = x_peers[0], x_peers[2]
    here = y * NZ + z
    g_at = [((here + k) % NG // NZ, (here + k) % NZ) for k in range(1, NG)]
    g_peers = [{"bank": bank_id(gy, x, gz)} for gy, gz in g_at]
    spot = x * ND + dp
    m_peers = []
    for k in range(1, NX * ND):
        other = (spot + k) % (NX * ND)
        m_peers.append({"dp": other % ND, "bank": bank_id(y, other // ND, z)})
    count = itertools.count()
    sent = []

    def channel():
        return sems.at[next(count)]

    def remote(src, dst, peer, out, into):
        return pltpu.make_async_remote_copy(
            src_ref=src,
            dst_ref=dst,
            send_sem=out,
            recv_sem=into,
            device_id=peer,
            device_id_type=MESH,
        )

    def take_all(sized, sem):
        pltpu.make_async_copy(sized, sized, sem).wait()

    def go(*copies):
        for copy in copies:
            copy.start()

    barrier = pltpu.get_barrier_semaphore()
    greeted = g_peers + m_peers
    for peer in greeted:
        pl.semaphore_signal(barrier, inc=1, device_id=peer, device_id_type=MESH)

    images, spots, channels = feat_ref.shape
    patches = patch_ref.shape[1]
    loads[0].wait()
    columns = jnp.transpose(patch_ref[...] - place * spots)
    loads[1].wait()
    for i in range(images):
        hit = columns[:, i : i + 1] == lax.broadcasted_iota(jnp.int32, (patches, spots), 1)
        picked = jnp.dot(hit.astype(BF16), feat_ref[i], preferred_element_type=F32).astype(BF16)
        picked = picked.reshape(patches // ROWS, CHUNKS, PART, channels)
        first = i * patches
        at = first // (NZ * ROWS)
        row = first % (NZ * ROWS) // CHUNKS
        for c in range(CHUNKS):
            fb[c, at % NX, at // NX, pl.ds(row, patches // CHUNKS), :] = picked[:, c].reshape(
                patches // CHUNKS, channels
            )
    pl.semaphore_wait(barrier, len(greeted))

    def over_x(b, a, u, m, c):
        out, across, last = channel(), channel(), channel()
        sent.append((b.at[pl.ds(0, 3)], out))
        return (
            [
                remote(b.at[xo, 0], a.at[0], plus, out, across),
                remote(b.at[xo, 1], a.at[1], minus, out, across),
            ],
            [
                remote(b.at[xp, 1], u.at[1], plus, out, last),
                remote(b.at[xm, 0], u.at[0], minus, out, last),
            ],
            [
                remote(m.at[0], c.at[0], plus, out, last),
                remote(m.at[1], c.at[1], minus, out, last),
            ],
            (a, across),
            (b.at[pl.ds(0, 2)], last),
        )

    def merge(b, a, m, copies):
        take_all(*copies[3])
        m[0] = a[0] + b[xp, 0]
        m[1] = a[1] + b[xm, 1]
        go(*copies[2])

    def x_total(b, u, c, s, copies):
        take_all(*copies[4])
        for h in range(NY):
            s[h] = (b[x, h] + u[h] + c[h]).reshape(s.shape[1:])

    def over_group(s, r):
        out, into = channel(), channel()
        sent.append((r, out))
        copies = [
            remote(s.at[gy, gz], r.at[k], peer, out, into)
            for k, ((gy, gz), peer) in enumerate(zip(g_at, g_peers))
        ]
        return copies, (r, into)

    def g_total(s, r, stage):
        take_all(*stage[1])
        total = s[y, z]
        for k in range(NG - 1):
            total = total + r[k]
        return total

    bank_dev = bank_ref.shape[0]
    wide = 2048

    def take(at, h):
        first = pl.multiple_of((h * NX + at) * NZ * ROWS, NZ * ROWS)
        rows = col[pl.ds(first, NZ * ROWS), :]
        acc[...] = jnp.zeros_like(acc)

        def some(j, _):
            start = pl.multiple_of(j * wide, wide)
            keys = lax.broadcasted_iota(jnp.int32, (NZ * ROWS, wide), 1) + start
            one = jnp.where(rows == keys, 1.0, 0.0).astype(BF16)
            acc[...] = acc[...] + jnp.dot(
                one, bank_ref[pl.ds(start, wide), :], preferred_element_type=F32
            )
            return 0

        lax.fori_loop(0, bank_dev // wide, some, 0)
        pb[at, h] = acc[...].astype(BF16)

    f = [over_x(fb.at[c], fa.at[c], fu.at[c], fm.at[c], fc.at[c]) for c in range(CHUNKS)]
    fg = [over_group(fs.at[c], fz.at[c]) for c in range(CHUNKS)]
    go(*f[0][0], *f[1][0], *f[0][1])
    loads[2].wait()
    columns = jnp.transpose(pos_ref[...] - place * bank_dev)
    for g in range(pos_ref.shape[0]):
        col[pl.ds(g * 128, 128), :] = columns[:, g : g + 1]
    loads[3].wait()
    p = over_x(pb, pa, pu, pm, pc)
    pg = over_group(ps, pz)
    take(xo, 0)
    take(xo, 1)
    merge(fb.at[0], fa.at[0], fm.at[0], f[0])
    take(xp, 1)
    merge(fb.at[1], fa.at[1], fm.at[1], f[1])
    go(*f[1][1])
    take(xm, 0)
    x_total(fb.at[0], fu.at[0], fc.at[0], fs.at[0], f[0])
    go(*fg[0][0])
    take(xp, 0)
    take(xm, 1)
    x_total(fb.at[1], fu.at[1], fc.at[1], fs.at[1], f[1])
    go(*fg[1][0])
    go(*p[0], *p[1])
    take(x, 0)
    take(x, 1)

    def unit_rows(own):
        scale = lax.rsqrt(jnp.mean(own * own, axis=-1, keepdims=True) + EPSILON)
        return own * scale / math.sqrt(channels)

    near_peers = [{"bank": bank_id(y, x, (z + k) % NZ)} for k in range(1, NZ)]
    far_peers = [{"bank": bank_id(1 - y, x, (z + k) % NZ)} for k in range(NZ)]

    def spread(c):
        out, near, far, one, two, relayed = (channel() for _ in range(6))
        sent.append((fz.at[c], out))
        more = channel()
        sent.append((fb.at[c, pl.ds(0, 3)], more))
        own = qa.at[c, x, y, z]
        mine, other = qa.at[c, x, y], qa.at[c, x, 1 - y]

        def forward(h):
            source = qa.at[c, (x + 3 + 2 * h) % NX, h]
            target = {"bank": bank_id(y, (x + 1 + 2 * h) % NX, z)}
            return remote(source, source, target, more, relayed)

        return {
            "z": [remote(own, own, peer, out, near) for peer in near_peers]
            + [remote(own, own, peer, out, far) for peer in far_peers],
            "z_in": (fz.at[c, pl.ds(0, NZ - 1)], near),
            "y_in": (fz.at[c, pl.ds(0, NZ)], far),
            "one": [remote(mine, mine, peer, more, one) for peer in (plus, minus)],
            "one_in": (fb.at[c, 0], one),
            "two": [remote(other, other, peer, more, two) for peer in (plus, minus)],
            "two_in": (fb.at[c, 0], two),
            "first": [forward(y)],
            "second": [forward(1 - y)],
            "relay_in": (fb.at[c, 0], relayed),
        }

    q = [spread(c) for c in range(CHUNKS)]

    def query_rows(c):
        own = g_total(fs.at[c], fz.at[c], fg[c]).astype(F32)
        raw[pl.ds(c * PART, PART), :] = own
        qa[c, x, y, z] = unit_rows(own).astype(BF16)
        go(*q[c]["z"])

    query_rows(0)
    merge(pb, pa, pm, p)
    query_rows(1)

    factor = 1.0 / (SOFTMAX_TEMP * math.log(2.0))
    block_keys = bank_dev // 2

    def half(c, at, j):
        query = qa[c, at].reshape(NY * HALF, channels)
        keys = bank_ref[pl.ds(j * block_keys, block_keys), :]
        dots = lax.dot_general(query, keys, (((1,), (1,)), ((), ())), preferred_element_type=F32)
        terms = jnp.exp2(dots * factor - factor)
        some = terms[:, :128]
        for lane in range(128, block_keys, 128):
            some = some + terms[:, lane : lane + 128]
        pushed = jnp.dot(terms.astype(BF16), keys, preferred_element_type=F32)
        if j == 0:
            tacc[...] = some
            acc[...] = pushed
        else:
            tacc[...] = tacc[...] + some
            acc[...] = acc[...] + pushed

    def finish(c, at):
        sums = jnp.sum(jnp.transpose(tacc[...]), axis=0, keepdims=True)
        for h in range(NY):
            ts[at, pl.ds(NY * c + h, 1), :] = sums[:, h * HALF : (h + 1) * HALF]

    def unit(c, at, between=lambda: None):
        half(c, at, 0)
        between()
        half(c, at, 1)
        finish(c, at)

    ts[...] = jnp.zeros_like(ts)
    w = [over_x(wb.at[c], wa.at[c], wu.at[c], wm.at[c], wc.at[c]) for c in range(CHUNKS)]
    wg = [over_group(ws.at[c], wz.at[c]) for c in range(CHUNKS)]

    def push_plus(c, between=lambda: None):
        unit(c, xp, between)
        wf[c, 0] = acc[pl.ds(0, HALF), :]
        wb[c, xp, 1] = acc[pl.ds(HALF, HALF), :].astype(BF16)
        go(w[c][1][0])

    def push_minus(c, between=lambda: None):
        unit(c, xm, between)
        wf[c, 1] = acc[pl.ds(HALF, HALF), :]
        wb[c, xm, 0] = acc[pl.ds(0, HALF), :].astype(BF16)

    def push_across(c):
        unit(c, xo)
        wb[c, xo, 0] = acc[pl.ds(0, HALF), :].astype(BF16)
        wb[c, xo, 1] = acc[pl.ds(HALF, HALF), :].astype(BF16)
        go(*w[c][0])

    def push_merged(c):
        take_all(*w[c][3])
        for h in range(NY):
            wm[c, h] = (wa[c, h].astype(F32) + wf[c, h]).astype(BF16)
        go(*w[c][2])

    def push_total(c):
        take_all(*w[c][4])
        for h in range(NY):
            part = wu[c, h].astype(F32) + wc[c, h].astype(F32)
            part = wo[c, h] + part.reshape(NZ, PART, channels)
            wo[c, h] = part
            ws[c, h] = part.astype(BF16)
        go(*wg[c][0])

    take_all(*q[0]["z_in"])
    go(*q[0]["one"])
    take_all(*q[0]["y_in"])
    go(*q[0]["two"])
    unit(0, x)
    wo[0] = acc[...].reshape(wo.shape[1:])
    take_all(*q[0]["one_in"])
    go(*q[0]["first"])
    take_all(*q[1]["z_in"])
    go(*q[1]["one"])
    take_all(*q[1]["y_in"])
    go(*q[1]["two"])
    half(1, x, 0)
    wo[1] = acc[...].reshape(wo.shape[1:])
    held[...] = tacc[...]
    take_all(*q[0]["two_in"])
    go(*q[0]["second"])
    x_total(pb, pu, pc, ps, p)
    go(*pg[0])

    def relay_first():
        take_all(*q[1]["one_in"])
        go(*q[1]["first"])

    def relay_second():
        take_all(*q[1]["two_in"])
        go(*q[1]["second"])

    push_plus(0, relay_first)
    push_minus(0, relay_second)
    go(w[0][1][1])
    take_all(*q[0]["relay_in"])
    push_across(0)
    take_all(*q[1]["relay_in"])
    push_across(1)
    push_plus(1, lambda: push_merged(0))
    positive = g_total(ps, pz, pg).astype(F32)
    query = qa[:, x, y, z].reshape(ROWS, channels).astype(F32)
    matched = jnp.sum(query * positive, axis=1, keepdims=True) / SOFTMAX_TEMP
    push_minus(1)
    t1_out, t1_in = channel(), channel()
    sent.append((tx, t1_out))
    go(
        *[
            remote(ts.at[(x + k) % NX], tx.at[k - 1], x_peers[k - 1], t1_out, t1_in)
            for k in range(1, NX)
        ]
    )
    push_merged(1)
    go(w[1][1][1])
    acc[...] = wo[1].reshape(acc.shape)
    tacc[...] = held[...]
    half(1, x, 1)
    finish(1, x)
    wo[1] = acc[...].reshape(wo.shape[1:])

    take_all(tx, t1_in)
    total = ts[x]
    for k in range(NX - 1):
        total = total + tx[k]
    line = lax.broadcasted_iota(jnp.int32, (8, 128), 0)
    tg[here] = jnp.where(
        line == 4, jnp.broadcast_to(jnp.sum(matched, axis=0, keepdims=True), (8, 128)), total
    )
    t2_out, t2_in = channel(), channel()
    others = tg.at[pl.ds(0, NG - 1)]
    sent.append((others, t2_out))
    go(*[remote(tg.at[here], tg.at[here], peer, t2_out, t2_in) for peer in g_peers])
    push_total(0)
    push_total(1)
    take_all(others, t2_in)
    total = tg[0]
    for k in range(1, NG):
        total = total + tg[k]
    lane = lax.broadcasted_iota(jnp.int32, (PART, HALF), 1)
    row = lax.broadcasted_iota(jnp.int32, (PART, HALF), 0)
    parts = []
    for c in range(CHUNKS):
        sums = jnp.where(y == 0, total[NY * c : NY * c + 1], total[NY * c + 1 : NY * c + 2])
        mine = jnp.where(lane == row + z * PART, jnp.broadcast_to(sums, (PART, HALF)), 0.0)
        parts.append(jnp.sum(mine, axis=1, keepdims=True))
    exponent_sum = jnp.concatenate(parts, axis=0)
    logs = jnp.sum(jnp.log(total[: NY * CHUNKS]), axis=0, keepdims=True)
    logs = jnp.sum(logs, axis=1, keepdims=True)
    quarter = logs + NG * ROWS / SOFTMAX_TEMP - total[4:5, :1]
    ms[spot] = jnp.broadcast_to(quarter, (8, 128))
    m1_out, m1_in = channel(), channel()
    rest = ms.at[pl.ds(0, NX * ND - 1)]
    sent.append((rest, m1_out))
    go(*[remote(ms.at[spot], ms.at[spot], peer, m1_out, m1_in) for peer in m_peers])

    loss = jnp.log(exponent_sum) + 1.0 / SOFTMAX_TEMP - matched
    diagonal = lax.broadcasted_iota(jnp.int32, (ROWS, ROWS), 0) == lax.broadcasted_iota(
        jnp.int32, (ROWS, ROWS), 1
    )
    loss_ref[...] = jnp.sum(
        jnp.where(diagonal, jnp.broadcast_to(loss, (ROWS, ROWS)), 0.0), axis=0, keepdims=True
    )
    own = raw[...]
    scale = lax.rsqrt(jnp.mean(own * own, axis=-1, keepdims=True) + EPSILON)
    for c in range(CHUNKS):
        take_all(*wg[c][1])
        weighted = wo[c, y, z]
        for k in range(NG - 1):
            weighted = weighted + wz[c, k].astype(F32)
        some = slice(c * PART, (c + 1) * PART)
        step = (weighted / exponent_sum[some] - positive[some]) / SOFTMAX_TEMP
        inner = jnp.mean(step * own[some], axis=-1, keepdims=True)
        s = scale[some]
        grad_ref[pl.ds(c * PART, PART), :] = (s / math.sqrt(channels)) * (
            step - own[some] * (s * s * inner)
        )
    take_all(rest, m1_in)
    losses = ms[0]
    for k in range(1, NX * ND):
        losses = losses + ms[k]
    mean_ref[...] = losses[:1] / count_all
    for sized, sem in sent:
        take_all(sized, sem)


def on_device(features, patch_index, positive_index, bank):
    images, hw_dev, channels = features.shape
    queries_dp = images * patch_index.shape[1]
    count_all = queries_dp * lax.axis_size("dp")
    positions = positive_index.reshape(-1, 128)

    def vmem(dtype, *shape):
        return pltpu.VMEM(shape, dtype)

    def chunked(*lead, rows):
        return [
            vmem(BF16, *lead, NX, NY, NZ * rows, channels),
            *[vmem(BF16, *lead, NY, NZ * rows, channels) for _ in range(4)],
            vmem(BF16, *lead, NY, NZ, rows, channels),
            vmem(BF16, *lead, NG - 1, rows, channels),
        ]

    scratch = [
        vmem(jnp.int32, *patch_index.shape),
        vmem(jnp.int32, *positions.shape),
        vmem(BF16, *features.shape),
        vmem(BF16, *bank.shape),
        *chunked(CHUNKS, rows=PART),
        *chunked(rows=ROWS),
        vmem(BF16, CHUNKS, NX, NY, NZ, PART, channels),
        vmem(F32, ROWS, channels),
        vmem(F32, CHUNKS, NY, HALF, channels),
        *chunked(CHUNKS, rows=PART)[:6],
        vmem(F32, CHUNKS, NY, NZ, PART, channels),
        vmem(BF16, CHUNKS, NG - 1, PART, channels),
        vmem(F32, NY * HALF, channels),
        vmem(F32, NY * HALF, 128),
        vmem(F32, NY * HALF, 128),
        vmem(F32, NX, 8, 128),
        vmem(F32, NX - 1, 8, 128),
        vmem(F32, NG, 8, 128),
        vmem(F32, NX * ND, 8, 128),
        vmem(jnp.int32, queries_dp, 1),
        pltpu.SemaphoreType.DMA((N_SEMS,)),
        pltpu.SemaphoreType.DMA((4,)),
    ]
    near, far = pl.BlockSpec(memory_space=pltpu.VMEM), pl.BlockSpec(memory_space=pl.ANY)
    loss, grad, mean = pl.pallas_call(
        lambda *refs: kernel(count_all, *refs),
        out_shape=(
            pltpu.VMEM((1, ROWS), F32),
            pltpu.VMEM((ROWS, channels), F32),
            pltpu.VMEM((1, 128), F32),
        ),
        in_specs=[far] * 4,
        out_specs=[near] * 3,
        scratch_shapes=scratch,
        compiler_params=pltpu.CompilerParams(
            collective_id=0, has_side_effects=True, vmem_limit_bytes=56 << 20
        ),
        name="patch_nce",
    )(patch_index, positions, features, bank)
    return (loss.reshape(ROWS), grad, mean[0, 0])


def solution(mesh):
    in_specs = (P("dp", "bank", None), P("dp", None), P("dp"), P("bank", None))
    out_specs = (P(("dp", "bank")), P(("dp", "bank"), None), P())
    return jax.shard_map(
        on_device, mesh=mesh, in_specs=in_specs, out_specs=out_specs, check_vma=False
    )
```

```python
import itertools
import math

import jax
import jax.numpy as jnp
from jax import lax
from jax.experimental import pallas as pl
from jax.experimental.pallas import tpu as pltpu
from jax.sharding import PartitionSpec as P

SOFTMAX_TEMP = 0.07
EPSILON = 1e-05
MESH = pl.DeviceIdType.MESH
F32, BF16 = jnp.float32, jnp.bfloat16

NY, NX, NZ, ND = 2, 4, 8, 4
NG = NY * NZ
ROWS = 32
CHUNKS = 2
PART = ROWS // CHUNKS
HALF = NZ * PART
N_SEMS = 48


def bank_id(y, x, z):
    return (y * NX + x) * NZ + z


def kernel(
    count_all,
    patch_hbm,
    pos_hbm,
    feat_hbm,
    bank_hbm,
    loss_ref,
    grad_ref,
    mean_ref,
    patch_ref, pos_ref, feat_ref, bank_ref,
    fb, fa, fu, fm, fc, fs, fz,
    pb, pa, pu, pm, pc, ps, pz,
    qa, raw,
    wf, wb, wa, wu, wm, wc, ws, wo, wz,
    acc, tacc, held,
    ts, tx, tg, ms,
    col,
    sems, lsem, heard,
):
    loads = [
        pltpu.make_async_copy(far, near, lsem.at[i])
        for i, (far, near) in enumerate(
            [(patch_hbm, patch_ref), (feat_hbm, feat_ref), (pos_hbm, pos_ref), (bank_hbm, bank_ref)]
        )
    ]
    for load in loads:
        load.start()
    place, dp = lax.axis_index("bank"), lax.axis_index("dp")
    y, x, z = place // (NX * NZ), (place // NZ) % NX, place % NZ
    xp, xo, xm = (x + 1) % NX, (x + 2) % NX, (x + 3) % NX
    x_peers = [{"bank": bank_id(y, (x + k) % NX, z)} for k in range(1, NX)]
    plus, minus = x_peers[0], x_peers[2]
    here = y * NZ + z
    g_at = [((here + k) % NG // NZ, (here + k) % NZ) for k in range(1, NG)]
    g_peers = [{"bank": bank_id(gy, x, gz)} for gy, gz in g_at]
    spot = x * ND + dp
    m_peers = []
    for k in range(1, NX * ND):
        other = (spot + k) % (NX * ND)
        m_peers.append({"dp": other % ND, "bank": bank_id(y, other // ND, z)})
    count = itertools.count()
    sent = []

    def channel():
        return sems.at[next(count)]

    def remote(src, dst, peer, out, into):
        return pltpu.make_async_remote_copy(
            src_ref=src,
            dst_ref=dst,
            send_sem=out,
            recv_sem=into,
            device_id=peer,
            device_id_type=MESH,
        )

    def take_all(sized, sem):
        pltpu.make_async_copy(sized, sized, sem).wait()

    def go(*copies):
        for copy in copies:
            copy.start()

    barrier = pltpu.get_barrier_semaphore()
    z_next = [{"bank": bank_id(y, x, (z + k) % NZ)} for k in (1, NZ - 1)]
    x_next = [plus, minus]
    greeted = x_next + z_next + [{"bank": bank_id(1 - y, x, z)}]
    greeted += [{"dp": (dp + k) % ND, "bank": place} for k in range(1, ND)]
    for peer in greeted:
        pl.semaphore_signal(barrier, inc=1, device_id=peer, device_id_type=MESH)

    def tell(i, peers):
        for peer in peers:
            pl.semaphore_signal(heard.at[i], inc=1, device_id=peer, device_id_type=MESH)

    def hear(i):
        pl.semaphore_wait(heard.at[i], 2)


    images, spots, channels = feat_ref.shape
    patches = patch_ref.shape[1]
    loads[0].wait()
    columns = jnp.transpose(patch_ref[...] - place * spots)
    loads[1].wait()
    for i in range(images):
        hit = columns[:, i : i + 1] == lax.broadcasted_iota(jnp.int32, (patches, spots), 1)
        picked = jnp.dot(hit.astype(BF16), feat_ref[i], preferred_element_type=F32).astype(BF16)
        picked = picked.reshape(patches // ROWS, CHUNKS, PART, channels)
        first = i * patches
        at = first // (NZ * ROWS)
        row = first % (NZ * ROWS) // CHUNKS
        for c in range(CHUNKS):
            fb[c, at % NX, at // NX, pl.ds(row, patches // CHUNKS), :] = picked[:, c].reshape(
                patches // CHUNKS, channels
            )
    pl.semaphore_wait(barrier, len(greeted))

    def over_x(b, a, u, m, c):
        out, across, last = channel(), channel(), channel()
        sent.append((b.at[pl.ds(0, 3)], out))
        return (
            [
                remote(b.at[xo, 0], a.at[0], plus, out, across),
                remote(b.at[xo, 1], a.at[1], minus, out, across),
            ],
            [
                remote(b.at[xp, 1], u.at[1], plus, out, last),
                remote(b.at[xm, 0], u.at[0], minus, out, last),
            ],
            [
                remote(m.at[0], c.at[0], plus, out, last),
                remote(m.at[1], c.at[1], minus, out, last),
            ],
            (a, across),
            (b.at[pl.ds(0, 2)], last),
        )

    def merge(b, a, m, copies):
        take_all(*copies[3])
        m[0] = a[0] + b[xp, 0]
        m[1] = a[1] + b[xm, 1]
        go(*copies[2])

    def x_total(b, u, c, s, copies):
        take_all(*copies[4])
        for h in range(NY):
            s[h] = (b[x, h] + u[h] + c[h]).reshape(s.shape[1:])

    def over_group(s, r):
        out, into = channel(), channel()
        sent.append((r, out))
        copies = [
            remote(s.at[gy, gz], r.at[k], peer, out, into)
            for k, ((gy, gz), peer) in enumerate(zip(g_at, g_peers))
        ]
        return copies, (r, into)

    def g_total(s, r, stage):
        take_all(*stage[1])
        total = s[y, z]
        for k in range(NG - 1):
            total = total + r[k]
        return total

    bank_dev = bank_ref.shape[0]
    wide = 2048

    def take(at, h):
        first = pl.multiple_of((h * NX + at) * NZ * ROWS, NZ * ROWS)
        rows = col[pl.ds(first, NZ * ROWS), :]
        acc[...] = jnp.zeros_like(acc)

        def some(j, _):
            start = pl.multiple_of(j * wide, wide)
            keys = lax.broadcasted_iota(jnp.int32, (NZ * ROWS, wide), 1) + start
            one = jnp.where(rows == keys, 1.0, 0.0).astype(BF16)
            acc[...] = acc[...] + jnp.dot(
                one, bank_ref[pl.ds(start, wide), :], preferred_element_type=F32
            )
            return 0

        lax.fori_loop(0, bank_dev // wide, some, 0)
        pb[at, h] = acc[...].astype(BF16)

    f = [over_x(fb.at[c], fa.at[c], fu.at[c], fm.at[c], fc.at[c]) for c in range(CHUNKS)]
    fg = [over_group(fs.at[c], fz.at[c]) for c in range(CHUNKS)]
    go(*f[0][0], *f[1][0], *f[0][1])
    tell(0, z_next)
    tell(4, x_next)
    loads[2].wait()
    columns = jnp.transpose(pos_ref[...] - place * bank_dev)
    for g in range(pos_ref.shape[0]):
        col[pl.ds(g * 128, 128), :] = columns[:, g : g + 1]
    loads[3].wait()
    p = over_x(pb, pa, pu, pm, pc)
    pg = over_group(ps, pz)
    take(xo, 0)
    hear(0)
    tell(1, z_next)
    hear(4)
    tell(5, x_next)
    take(xo, 1)
    hear(1)
    tell(2, z_next)
    merge(fb.at[0], fa.at[0], fm.at[0], f[0])
    take(xp, 1)
    hear(2)
    tell(3, z_next)
    merge(fb.at[1], fa.at[1], fm.at[1], f[1])
    go(*f[1][1])
    take(xm, 0)
    hear(3)
    hear(5)
    x_total(fb.at[0], fu.at[0], fc.at[0], fs.at[0], f[0])
    go(*fg[0][0])
    take(xp, 0)
    take(xm, 1)
    x_total(fb.at[1], fu.at[1], fc.at[1], fs.at[1], f[1])
    go(*fg[1][0])
    go(*p[0], *p[1])
    take(x, 0)
    take(x, 1)

    def unit_rows(own):
        scale = lax.rsqrt(jnp.mean(own * own, axis=-1, keepdims=True) + EPSILON)
        return own * scale / math.sqrt(channels)

    near_peers = [{"bank": bank_id(y, x, (z + k) % NZ)} for k in range(1, NZ)]
    far_peers = [{"bank": bank_id(1 - y, x, (z + k) % NZ)} for k in range(NZ)]

    def spread(c):
        out, near, far, one, two, relayed = (channel() for _ in range(6))
        sent.append((fz.at[c], out))
        more = channel()
        sent.append((fb.at[c, pl.ds(0, 3)], more))
        own = qa.at[c, x, y, z]
        mine, other = qa.at[c, x, y], qa.at[c, x, 1 - y]

        def forward(h):
            source = qa.at[c, (x + 3 + 2 * h) % NX, h]
            target = {"bank": bank_id(y, (x + 1 + 2 * h) % NX, z)}
            return remote(source, source, target, more, relayed)

        return {
            "z": [remote(own, own, peer, out, near) for peer in near_peers]
            + [remote(own, own, peer, out, far) for peer in far_peers],
            "z_in": (fz.at[c, pl.ds(0, NZ - 1)], near),
            "y_in": (fz.at[c, pl.ds(0, NZ)], far),
            "one": [remote(mine, mine, peer, more, one) for peer in (plus, minus)],
            "one_in": (fb.at[c, 0], one),
            "two": [remote(other, other, peer, more, two) for peer in (plus, minus)],
            "two_in": (fb.at[c, 0], two),
            "first": [forward(y)],
            "second": [forward(1 - y)],
            "relay_in": (fb.at[c, 0], relayed),
        }

    q = [spread(c) for c in range(CHUNKS)]

    def query_rows(c):
        own = g_total(fs.at[c], fz.at[c], fg[c]).astype(F32)
        raw[pl.ds(c * PART, PART), :] = own
        qa[c, x, y, z] = unit_rows(own).astype(BF16)
        go(*q[c]["z"])

    query_rows(0)
    merge(pb, pa, pm, p)
    query_rows(1)

    factor = 1.0 / (SOFTMAX_TEMP * math.log(2.0))
    block_keys = bank_dev // 2

    def half(c, at, j):
        query = qa[c, at].reshape(NY * HALF, channels)
        keys = bank_ref[pl.ds(j * block_keys, block_keys), :]
        dots = lax.dot_general(query, keys, (((1,), (1,)), ((), ())), preferred_element_type=F32)
        terms = jnp.exp2(dots * factor - factor)
        some = terms[:, :128]
        for lane in range(128, block_keys, 128):
            some = some + terms[:, lane : lane + 128]
        pushed = jnp.dot(terms.astype(BF16), keys, preferred_element_type=F32)
        if j == 0:
            tacc[...] = some
            acc[...] = pushed
        else:
            tacc[...] = tacc[...] + some
            acc[...] = acc[...] + pushed

    def finish(c, at):
        sums = jnp.sum(jnp.transpose(tacc[...]), axis=0, keepdims=True)
        for h in range(NY):
            ts[at, pl.ds(NY * c + h, 1), :] = sums[:, h * HALF : (h + 1) * HALF]

    def unit(c, at, between=lambda: None):
        half(c, at, 0)
        between()
        half(c, at, 1)
        finish(c, at)

    ts[...] = jnp.zeros_like(ts)
    w = [over_x(wb.at[c], wa.at[c], wu.at[c], wm.at[c], wc.at[c]) for c in range(CHUNKS)]
    wg = [over_group(ws.at[c], wz.at[c]) for c in range(CHUNKS)]

    def push_plus(c, between=lambda: None):
        unit(c, xp, between)
        wf[c, 0] = acc[pl.ds(0, HALF), :]
        wb[c, xp, 1] = acc[pl.ds(HALF, HALF), :].astype(BF16)
        go(w[c][1][0])

    def push_minus(c, between=lambda: None):
        unit(c, xm, between)
        wf[c, 1] = acc[pl.ds(HALF, HALF), :]
        wb[c, xm, 0] = acc[pl.ds(0, HALF), :].astype(BF16)

    def push_halves(c):
        wb[c, xo, 0] = acc[pl.ds(0, HALF), :].astype(BF16)
        wb[c, xo, 1] = acc[pl.ds(HALF, HALF), :].astype(BF16)
        go(*w[c][0])

    def push_merged(c):
        take_all(*w[c][3])
        for h in range(NY):
            wm[c, h] = (wa[c, h].astype(F32) + wf[c, h]).astype(BF16)
        go(*w[c][2])

    def push_total(c):
        take_all(*w[c][4])
        for h in range(NY):
            part = wu[c, h].astype(F32) + wc[c, h].astype(F32)
            part = wo[c, h] + part.reshape(NZ, PART, channels)
            wo[c, h] = part
            ws[c, h] = part.astype(BF16)
        go(*wg[c][0])

    take_all(*q[0]["z_in"])
    go(*q[0]["one"])
    take_all(*q[0]["y_in"])
    go(*q[0]["two"])
    unit(0, x)
    wo[0] = acc[...].reshape(wo.shape[1:])
    take_all(*q[1]["z_in"])
    go(*q[1]["one"])
    take_all(*q[1]["y_in"])
    go(*q[1]["two"])
    half(1, x, 0)
    wo[1] = acc[...].reshape(wo.shape[1:])
    held[...] = tacc[...]
    take_all(*q[0]["one_in"])
    go(*q[0]["first"])
    take_all(*q[0]["two_in"])
    go(*q[0]["second"])
    x_total(pb, pu, pc, ps, p)
    go(*pg[0])
    push_plus(0)
    push_minus(0)
    take_all(*q[1]["one_in"])
    go(*q[1]["first"])
    go(w[0][1][1])
    take_all(*q[1]["two_in"])
    go(*q[1]["second"])
    push_plus(1)
    take_all(*q[0]["relay_in"])
    unit(0, xo)
    push_halves(0)
    take_all(*q[1]["relay_in"])
    t1_out, t1_in = channel(), channel()
    sent.append((tx, t1_out))
    t1 = [
        remote(ts.at[(x + k) % NX], tx.at[k - 1], x_peers[k - 1], t1_out, t1_in)
        for k in range(1, NX)
    ]
    unit(1, xo)
    go(t1[1], t1[0])
    push_halves(1)
    positive = g_total(ps, pz, pg).astype(F32)
    query = qa[:, x, y, z].reshape(ROWS, channels).astype(F32)
    matched = jnp.sum(query * positive, axis=1, keepdims=True) / SOFTMAX_TEMP
    push_minus(1, lambda: push_merged(0))
    go(t1[2])
    go(w[1][1][1])
    acc[...] = wo[1].reshape(acc.shape)
    tacc[...] = held[...]
    half(1, x, 1)
    finish(1, x)
    wo[1] = acc[...].reshape(wo.shape[1:])
    push_merged(1)

    take_all(tx, t1_in)
    total = ts[x]
    for k in range(NX - 1):
        total = total + tx[k]
    line = lax.broadcasted_iota(jnp.int32, (8, 128), 0)
    tg[here] = jnp.where(
        line == 4, jnp.broadcast_to(jnp.sum(matched, axis=0, keepdims=True), (8, 128)), total
    )
    t2_out, t2_in = channel(), channel()
    others = tg.at[pl.ds(0, NG - 1)]
    sent.append((others, t2_out))
    go(*[remote(tg.at[here], tg.at[here], peer, t2_out, t2_in) for peer in g_peers])
    push_total(0)
    push_total(1)
    take_all(others, t2_in)
    total = tg[0]
    for k in range(1, NG):
        total = total + tg[k]
    lane = lax.broadcasted_iota(jnp.int32, (PART, HALF), 1)
    row = lax.broadcasted_iota(jnp.int32, (PART, HALF), 0)
    parts = []
    for c in range(CHUNKS):
        sums = jnp.where(y == 0, total[NY * c : NY * c + 1], total[NY * c + 1 : NY * c + 2])
        mine = jnp.where(lane == row + z * PART, jnp.broadcast_to(sums, (PART, HALF)), 0.0)
        parts.append(jnp.sum(mine, axis=1, keepdims=True))
    exponent_sum = jnp.concatenate(parts, axis=0)
    logs = jnp.sum(jnp.log(total[: NY * CHUNKS]), axis=0, keepdims=True)
    logs = jnp.sum(logs, axis=1, keepdims=True)
    quarter = logs + NG * ROWS / SOFTMAX_TEMP - total[4:5, :1]
    ms[spot] = jnp.broadcast_to(quarter, (8, 128))
    m1_out, m1_in = channel(), channel()
    rest = ms.at[pl.ds(0, NX * ND - 1)]
    sent.append((rest, m1_out))
    go(*[remote(ms.at[spot], ms.at[spot], peer, m1_out, m1_in) for peer in m_peers])

    loss = jnp.log(exponent_sum) + 1.0 / SOFTMAX_TEMP - matched
    diagonal = lax.broadcasted_iota(jnp.int32, (ROWS, ROWS), 0) == lax.broadcasted_iota(
        jnp.int32, (ROWS, ROWS), 1
    )
    loss_ref[...] = jnp.sum(
        jnp.where(diagonal, jnp.broadcast_to(loss, (ROWS, ROWS)), 0.0), axis=0, keepdims=True
    )
    own = raw[...]
    scale = lax.rsqrt(jnp.mean(own * own, axis=-1, keepdims=True) + EPSILON)
    for c in range(CHUNKS):
        take_all(*wg[c][1])
        weighted = wo[c, y, z]
        for k in range(NG - 1):
            weighted = weighted + wz[c, k].astype(F32)
        some = slice(c * PART, (c + 1) * PART)
        step = (weighted / exponent_sum[some] - positive[some]) / SOFTMAX_TEMP
        inner = jnp.mean(step * own[some], axis=-1, keepdims=True)
        s = scale[some]
        grad_ref[pl.ds(c * PART, PART), :] = (s / math.sqrt(channels)) * (
            step - own[some] * (s * s * inner)
        )
    take_all(rest, m1_in)
    losses = ms[0]
    for k in range(1, NX * ND):
        losses = losses + ms[k]
    mean_ref[...] = losses[:1] / count_all
    for sized, sem in sent:
        take_all(sized, sem)


def on_device(features, patch_index, positive_index, bank):
    images, hw_dev, channels = features.shape
    queries_dp = images * patch_index.shape[1]
    count_all = queries_dp * lax.axis_size("dp")
    positions = positive_index.reshape(-1, 128)

    def vmem(dtype, *shape):
        return pltpu.VMEM(shape, dtype)

    def chunked(*lead, rows):
        return [
            vmem(BF16, *lead, NX, NY, NZ * rows, channels),
            *[vmem(BF16, *lead, NY, NZ * rows, channels) for _ in range(4)],
            vmem(BF16, *lead, NY, NZ, rows, channels),
            vmem(BF16, *lead, NG - 1, rows, channels),
        ]

    scratch = [
        vmem(jnp.int32, *patch_index.shape),
        vmem(jnp.int32, *positions.shape),
        vmem(BF16, *features.shape),
        vmem(BF16, *bank.shape),
        *chunked(CHUNKS, rows=PART),
        *chunked(rows=ROWS),
        vmem(BF16, CHUNKS, NX, NY, NZ, PART, channels),
        vmem(F32, ROWS, channels),
        vmem(F32, CHUNKS, NY, HALF, channels),
        *chunked(CHUNKS, rows=PART)[:6],
        vmem(F32, CHUNKS, NY, NZ, PART, channels),
        vmem(BF16, CHUNKS, NG - 1, PART, channels),
        vmem(F32, NY * HALF, channels),
        vmem(F32, NY * HALF, 128),
        vmem(F32, NY * HALF, 128),
        vmem(F32, NX, 8, 128),
        vmem(F32, NX - 1, 8, 128),
        vmem(F32, NG, 8, 128),
        vmem(F32, NX * ND, 8, 128),
        vmem(jnp.int32, queries_dp, 1),
        pltpu.SemaphoreType.DMA((N_SEMS,)),
        pltpu.SemaphoreType.DMA((4,)),
        pltpu.SemaphoreType.REGULAR((6,)),
    ]
    near, far = pl.BlockSpec(memory_space=pltpu.VMEM), pl.BlockSpec(memory_space=pl.ANY)
    loss, grad, mean = pl.pallas_call(
        lambda *refs: kernel(count_all, *refs),
        out_shape=(
            pltpu.VMEM((1, ROWS), F32),
            pltpu.VMEM((ROWS, channels), F32),
            pltpu.VMEM((1, 128), F32),
        ),
        in_specs=[far] * 4,
        out_specs=[near] * 3,
        scratch_shapes=scratch,
        compiler_params=pltpu.CompilerParams(
            collective_id=0, has_side_effects=True, vmem_limit_bytes=56 << 20
        ),
        name="patch_nce",
    )(patch_index, positions, features, bank)
    return (loss.reshape(ROWS), grad, mean[0, 0])


def solution(mesh):
    in_specs = (P("dp", "bank", None), P("dp", None), P("dp"), P("bank", None))
    out_specs = (P(("dp", "bank")), P(("dp", "bank"), None), P())
    return jax.shard_map(
        on_device, mesh=mesh, in_specs=in_specs, out_specs=out_specs, check_vma=False
    )
```

```python
import itertools
import math

import jax
import jax.numpy as jnp
from jax import lax
from jax.experimental import pallas as pl
from jax.experimental.pallas import tpu as pltpu
from jax.sharding import PartitionSpec as P

SOFTMAX_TEMP = 0.07
EPSILON = 1e-05
MESH = pl.DeviceIdType.MESH
F32, BF16 = jnp.float32, jnp.bfloat16

NY, NX, NZ, ND = 2, 4, 8, 4
NG = NY * NZ
ROWS = 32
CHUNKS = 2
PART = ROWS // CHUNKS
HALF = NZ * PART
N_SEMS = 48


def bank_id(y, x, z):
    return (y * NX + x) * NZ + z


def kernel(
    count_all,
    patch_hbm,
    pos_hbm,
    feat_hbm,
    bank_hbm,
    loss_ref,
    grad_ref,
    mean_ref,
    patch_ref, pos_ref, feat_ref, bank_ref,
    fb, fa, fu, fm, fc, fs, fz,
    pb, pa, pu, pm, pc, ps, pz,
    qa, raw,
    wf, wb, wa, wu, wm, wc, ws, wo, wz,
    acc, tacc, held,
    ts, tx, tg, ms,
    col,
    sems, lsem, heard,
):
    loads = [
        pltpu.make_async_copy(far, near, lsem.at[i])
        for i, (far, near) in enumerate(
            [(patch_hbm, patch_ref), (feat_hbm, feat_ref), (pos_hbm, pos_ref), (bank_hbm, bank_ref)]
        )
    ]
    for load in loads:
        load.start()
    place, dp = lax.axis_index("bank"), lax.axis_index("dp")
    y, x, z = place // (NX * NZ), (place // NZ) % NX, place % NZ
    xp, xo, xm = (x + 1) % NX, (x + 2) % NX, (x + 3) % NX
    x_peers = [{"bank": bank_id(y, (x + k) % NX, z)} for k in range(1, NX)]
    plus, minus = x_peers[0], x_peers[2]
    here = y * NZ + z
    g_at = [((here + k) % NG // NZ, (here + k) % NZ) for k in range(1, NG)]
    g_peers = [{"bank": bank_id(gy, x, gz)} for gy, gz in g_at]
    spot = x * ND + dp
    m_peers = []
    for k in range(1, NX * ND):
        other = (spot + k) % (NX * ND)
        m_peers.append({"dp": other % ND, "bank": bank_id(y, other // ND, z)})
    count = itertools.count()
    sent = []

    def channel():
        return sems.at[next(count)]

    def remote(src, dst, peer, out, into):
        return pltpu.make_async_remote_copy(
            src_ref=src,
            dst_ref=dst,
            send_sem=out,
            recv_sem=into,
            device_id=peer,
            device_id_type=MESH,
        )

    def take_all(sized, sem):
        pltpu.make_async_copy(sized, sized, sem).wait()

    def go(*copies):
        for copy in copies:
            copy.start()

    barrier = pltpu.get_barrier_semaphore()
    z_next = [{"bank": bank_id(y, x, (z + k) % NZ)} for k in (1, NZ - 1)]
    x_next = [plus, minus]
    greeted = x_next + z_next + [{"bank": bank_id(1 - y, x, z)}]
    greeted += [{"dp": (dp + k) % ND, "bank": place} for k in range(1, ND)]
    for peer in greeted:
        pl.semaphore_signal(barrier, inc=1, device_id=peer, device_id_type=MESH)

    def tell(i, peers):
        for peer in peers:
            pl.semaphore_signal(heard.at[i], inc=1, device_id=peer, device_id_type=MESH)

    def hear(i):
        pl.semaphore_wait(heard.at[i], 2)


    images, spots, channels = feat_ref.shape
    patches = patch_ref.shape[1]
    loads[0].wait()
    columns = jnp.transpose(patch_ref[...] - place * spots)
    loads[1].wait()
    for i in range(images):
        hit = columns[:, i : i + 1] == lax.broadcasted_iota(jnp.int32, (patches, spots), 1)
        picked = jnp.dot(hit.astype(BF16), feat_ref[i], preferred_element_type=F32).astype(BF16)
        picked = picked.reshape(patches // ROWS, CHUNKS, PART, channels)
        first = i * patches
        at = first // (NZ * ROWS)
        row = first % (NZ * ROWS) // CHUNKS
        for c in range(CHUNKS):
            fb[c, at % NX, at // NX, pl.ds(row, patches // CHUNKS), :] = picked[:, c].reshape(
                patches // CHUNKS, channels
            )
    pl.semaphore_wait(barrier, len(greeted))

    def over_x(b, a, u, m, c):
        out, across, last = channel(), channel(), channel()
        sent.append((b.at[pl.ds(0, 3)], out))
        return (
            [
                remote(b.at[xo, 0], a.at[0], plus, out, across),
                remote(b.at[xo, 1], a.at[1], minus, out, across),
            ],
            [
                remote(b.at[xp, 1], u.at[1], plus, out, last),
                remote(b.at[xm, 0], u.at[0], minus, out, last),
            ],
            [
                remote(m.at[0], c.at[0], plus, out, last),
                remote(m.at[1], c.at[1], minus, out, last),
            ],
            (a, across),
            (b.at[pl.ds(0, 2)], last),
        )

    def merge(b, a, m, copies):
        take_all(*copies[3])
        m[0] = a[0] + b[xp, 0]
        m[1] = a[1] + b[xm, 1]
        go(*copies[2])

    def x_total(b, u, c, s, copies):
        take_all(*copies[4])
        for h in range(NY):
            s[h] = (b[x, h] + u[h] + c[h]).reshape(s.shape[1:])

    def over_group(s, r):
        out, into = channel(), channel()
        sent.append((r, out))
        copies = [
            remote(s.at[gy, gz], r.at[k], peer, out, into)
            for k, ((gy, gz), peer) in enumerate(zip(g_at, g_peers))
        ]
        return copies, (r, into)

    def g_total(s, r, stage):
        take_all(*stage[1])
        total = s[y, z]
        for k in range(NG - 1):
            total = total + r[k]
        return total

    bank_dev = bank_ref.shape[0]
    wide = 2048

    def take(at, h):
        first = pl.multiple_of((h * NX + at) * NZ * ROWS, NZ * ROWS)
        rows = col[pl.ds(first, NZ * ROWS), :]
        acc[...] = jnp.zeros_like(acc)

        def some(j, _):
            start = pl.multiple_of(j * wide, wide)
            keys = lax.broadcasted_iota(jnp.int32, (NZ * ROWS, wide), 1) + start
            one = jnp.where(rows == keys, 1.0, 0.0).astype(BF16)
            acc[...] = acc[...] + jnp.dot(
                one, bank_ref[pl.ds(start, wide), :], preferred_element_type=F32
            )
            return 0

        lax.fori_loop(0, bank_dev // wide, some, 0)
        pb[at, h] = acc[...].astype(BF16)

    f = [over_x(fb.at[c], fa.at[c], fu.at[c], fm.at[c], fc.at[c]) for c in range(CHUNKS)]
    fg = [over_group(fs.at[c], fz.at[c]) for c in range(CHUNKS)]
    go(*f[0][0], *f[1][0], *f[0][1])
    tell(0, z_next)
    tell(4, x_next)
    loads[2].wait()
    columns = jnp.transpose(pos_ref[...] - place * bank_dev)
    for g in range(pos_ref.shape[0]):
        col[pl.ds(g * 128, 128), :] = columns[:, g : g + 1]
    loads[3].wait()
    p = over_x(pb, pa, pu, pm, pc)
    pg = over_group(ps, pz)
    take(xo, 0)
    hear(0)
    tell(1, z_next)
    hear(4)
    tell(5, x_next)
    take(xo, 1)
    hear(1)
    tell(2, z_next)
    merge(fb.at[0], fa.at[0], fm.at[0], f[0])
    take(xp, 1)
    hear(2)
    tell(3, z_next)
    merge(fb.at[1], fa.at[1], fm.at[1], f[1])
    go(*f[1][1])
    take(xm, 0)
    hear(3)
    hear(5)
    x_total(fb.at[0], fu.at[0], fc.at[0], fs.at[0], f[0])
    go(*fg[0][0])
    take(xp, 0)
    take(xm, 1)
    x_total(fb.at[1], fu.at[1], fc.at[1], fs.at[1], f[1])
    go(*fg[1][0])
    go(*p[0], *p[1])
    take(x, 0)
    take(x, 1)

    def unit_rows(own):
        scale = lax.rsqrt(jnp.mean(own * own, axis=-1, keepdims=True) + EPSILON)
        return own * scale / math.sqrt(channels)

    near_peers = [{"bank": bank_id(y, x, (z + k) % NZ)} for k in range(1, NZ)]
    far_peers = [{"bank": bank_id(1 - y, x, (z + k) % NZ)} for k in range(NZ)]

    def spread(c):
        out, near, far, one, two, relayed = (channel() for _ in range(6))
        sent.append((fz.at[c], out))
        more = channel()
        sent.append((fb.at[c, pl.ds(0, 3)], more))
        own = qa.at[c, x, y, z]
        mine, other = qa.at[c, x, y], qa.at[c, x, 1 - y]

        def forward(h):
            source = qa.at[c, (x + 3 + 2 * h) % NX, h]
            target = {"bank": bank_id(y, (x + 1 + 2 * h) % NX, z)}
            return remote(source, source, target, more, relayed)

        return {
            "z": [remote(own, own, peer, out, near) for peer in near_peers]
            + [remote(own, own, peer, out, far) for peer in far_peers],
            "z_in": (fz.at[c, pl.ds(0, NZ - 1)], near),
            "y_in": (fz.at[c, pl.ds(0, NZ)], far),
            "one": [remote(mine, mine, peer, more, one) for peer in (plus, minus)],
            "one_in": (fb.at[c, 0], one),
            "two": [remote(other, other, peer, more, two) for peer in (plus, minus)],
            "two_in": (fb.at[c, 0], two),
            "first": [forward(y)],
            "second": [forward(1 - y)],
            "relay_in": (fb.at[c, 0], relayed),
        }

    q = [spread(c) for c in range(CHUNKS)]

    def query_rows(c):
        own = g_total(fs.at[c], fz.at[c], fg[c]).astype(F32)
        raw[pl.ds(c * PART, PART), :] = own
        qa[c, x, y, z] = unit_rows(own).astype(BF16)
        go(*q[c]["z"])

    query_rows(0)
    merge(pb, pa, pm, p)
    query_rows(1)

    factor = 1.0 / (SOFTMAX_TEMP * math.log(2.0))
    block_keys = bank_dev // 2

    def half(c, at, j):
        query = qa[c, at].reshape(NY * HALF, channels)
        keys = bank_ref[pl.ds(j * block_keys, block_keys), :]
        dots = lax.dot_general(query, keys, (((1,), (1,)), ((), ())), preferred_element_type=F32)
        terms = jnp.exp2(dots * factor - factor)
        some = terms[:, :128]
        for lane in range(128, block_keys, 128):
            some = some + terms[:, lane : lane + 128]
        pushed = jnp.dot(terms.astype(BF16), keys, preferred_element_type=F32)
        if j == 0:
            tacc[...] = some
            acc[...] = pushed
        else:
            tacc[...] = tacc[...] + some
            acc[...] = acc[...] + pushed

    def finish(c, at):
        sums = jnp.sum(jnp.transpose(tacc[...]), axis=0, keepdims=True)
        for h in range(NY):
            ts[at, pl.ds(NY * c + h, 1), :] = sums[:, h * HALF : (h + 1) * HALF]

    def unit(c, at, between=lambda: None):
        half(c, at, 0)
        between()
        half(c, at, 1)
        finish(c, at)

    ts[...] = jnp.zeros_like(ts)
    w = [over_x(wb.at[c], wa.at[c], wu.at[c], wm.at[c], wc.at[c]) for c in range(CHUNKS)]
    wg = [over_group(ws.at[c], wz.at[c]) for c in range(CHUNKS)]

    def push_plus(c, between=lambda: None):
        unit(c, xp, between)
        wf[c, 0] = acc[pl.ds(0, HALF), :]
        wb[c, xp, 1] = acc[pl.ds(HALF, HALF), :].astype(BF16)
        go(w[c][1][0])

    def push_minus(c, between=lambda: None):
        unit(c, xm, between)
        wf[c, 1] = acc[pl.ds(HALF, HALF), :]
        wb[c, xm, 0] = acc[pl.ds(0, HALF), :].astype(BF16)

    def push_halves(c):
        wb[c, xo, 0] = acc[pl.ds(0, HALF), :].astype(BF16)
        wb[c, xo, 1] = acc[pl.ds(HALF, HALF), :].astype(BF16)
        go(*w[c][0])

    def push_merged(c):
        take_all(*w[c][3])
        for h in range(NY):
            wm[c, h] = (wa[c, h].astype(F32) + wf[c, h]).astype(BF16)
        go(*w[c][2])

    def push_total(c):
        take_all(*w[c][4])
        for h in range(NY):
            part = wu[c, h].astype(F32) + wc[c, h].astype(F32)
            part = wo[c, h] + part.reshape(NZ, PART, channels)
            wo[c, h] = part
            ws[c, h] = part.astype(BF16)
        go(*wg[c][0])

    take_all(*q[0]["z_in"])
    go(*q[0]["one"])
    take_all(*q[0]["y_in"])
    go(*q[0]["two"])
    unit(0, x)
    wo[0] = acc[...].reshape(wo.shape[1:])
    take_all(*q[1]["z_in"])
    go(*q[1]["one"])
    take_all(*q[1]["y_in"])
    go(*q[1]["two"])
    half(1, x, 0)
    wo[1] = acc[...].reshape(wo.shape[1:])
    held[...] = tacc[...]
    take_all(*q[0]["one_in"])
    go(*q[0]["first"])
    take_all(*q[0]["two_in"])
    go(*q[0]["second"])
    x_total(pb, pu, pc, ps, p)
    go(*pg[0])
    push_plus(0)
    push_minus(0)
    take_all(*q[1]["one_in"])
    go(*q[1]["first"])
    go(w[0][1][1])
    take_all(*q[1]["two_in"])
    go(*q[1]["second"])
    push_plus(1)
    take_all(*q[0]["relay_in"])
    unit(0, xo)
    push_halves(0)
    take_all(*q[1]["relay_in"])
    t1_out, t1_in = channel(), channel()
    sent.append((tx, t1_out))
    t1 = [
        remote(ts.at[(x + k) % NX], tx.at[k - 1], x_peers[k - 1], t1_out, t1_in)
        for k in range(1, NX)
    ]
    unit(1, xo)
    go(t1[1], t1[0])
    push_halves(1)
    positive = g_total(ps, pz, pg).astype(F32)
    query = qa[:, x, y, z].reshape(ROWS, channels).astype(F32)
    matched = jnp.sum(query * positive, axis=1, keepdims=True) / SOFTMAX_TEMP
    push_minus(1)
    go(t1[2])
    push_merged(0)
    go(w[1][1][1])
    acc[...] = wo[1].reshape(acc.shape)
    tacc[...] = held[...]
    half(1, x, 1)
    finish(1, x)
    wo[1] = acc[...].reshape(wo.shape[1:])

    take_all(tx, t1_in)
    total = ts[x]
    for k in range(NX - 1):
        total = total + tx[k]
    line = lax.broadcasted_iota(jnp.int32, (8, 128), 0)
    tg[here] = jnp.where(
        line == 4, jnp.broadcast_to(jnp.sum(matched, axis=0, keepdims=True), (8, 128)), total
    )
    t2_out, t2_in = channel(), channel()
    others = tg.at[pl.ds(0, NG - 1)]
    sent.append((others, t2_out))
    go(*[remote(tg.at[here], tg.at[here], peer, t2_out, t2_in) for peer in g_peers])
    push_merged(1)
    push_total(0)
    push_total(1)
    take_all(others, t2_in)
    total = tg[0]
    for k in range(1, NG):
        total = total + tg[k]
    lane = lax.broadcasted_iota(jnp.int32, (PART, HALF), 1)
    row = lax.broadcasted_iota(jnp.int32, (PART, HALF), 0)
    parts = []
    for c in range(CHUNKS):
        sums = jnp.where(y == 0, total[NY * c : NY * c + 1], total[NY * c + 1 : NY * c + 2])
        mine = jnp.where(lane == row + z * PART, jnp.broadcast_to(sums, (PART, HALF)), 0.0)
        parts.append(jnp.sum(mine, axis=1, keepdims=True))
    exponent_sum = jnp.concatenate(parts, axis=0)
    logs = jnp.sum(jnp.log(total[: NY * CHUNKS]), axis=0, keepdims=True)
    logs = jnp.sum(logs, axis=1, keepdims=True)
    quarter = logs + NG * ROWS / SOFTMAX_TEMP - total[4:5, :1]
    ms[spot] = jnp.broadcast_to(quarter, (8, 128))
    m1_out, m1_in = channel(), channel()
    rest = ms.at[pl.ds(0, NX * ND - 1)]
    sent.append((rest, m1_out))
    go(*[remote(ms.at[spot], ms.at[spot], peer, m1_out, m1_in) for peer in m_peers])

    loss = jnp.log(exponent_sum) + 1.0 / SOFTMAX_TEMP - matched
    diagonal = lax.broadcasted_iota(jnp.int32, (ROWS, ROWS), 0) == lax.broadcasted_iota(
        jnp.int32, (ROWS, ROWS), 1
    )
    loss_ref[...] = jnp.sum(
        jnp.where(diagonal, jnp.broadcast_to(loss, (ROWS, ROWS)), 0.0), axis=0, keepdims=True
    )
    own = raw[...]
    scale = lax.rsqrt(jnp.mean(own * own, axis=-1, keepdims=True) + EPSILON)
    for c in range(CHUNKS):
        take_all(*wg[c][1])
        weighted = wo[c, y, z]
        for k in range(NG - 1):
            weighted = weighted + wz[c, k].astype(F32)
        some = slice(c * PART, (c + 1) * PART)
        step = (weighted / exponent_sum[some] - positive[some]) / SOFTMAX_TEMP
        inner = jnp.mean(step * own[some], axis=-1, keepdims=True)
        s = scale[some]
        grad_ref[pl.ds(c * PART, PART), :] = (s / math.sqrt(channels)) * (
            step - own[some] * (s * s * inner)
        )
    take_all(rest, m1_in)
    losses = ms[0]
    for k in range(1, NX * ND):
        losses = losses + ms[k]
    mean_ref[...] = losses[:1] / count_all
    for sized, sem in sent:
        take_all(sized, sem)


def on_device(features, patch_index, positive_index, bank):
    images, hw_dev, channels = features.shape
    queries_dp = images * patch_index.shape[1]
    count_all = queries_dp * lax.axis_size("dp")
    positions = positive_index.reshape(-1, 128)

    def vmem(dtype, *shape):
        return pltpu.VMEM(shape, dtype)

    def chunked(*lead, rows):
        return [
            vmem(BF16, *lead, NX, NY, NZ * rows, channels),
            *[vmem(BF16, *lead, NY, NZ * rows, channels) for _ in range(4)],
            vmem(BF16, *lead, NY, NZ, rows, channels),
            vmem(BF16, *lead, NG - 1, rows, channels),
        ]

    scratch = [
        vmem(jnp.int32, *patch_index.shape),
        vmem(jnp.int32, *positions.shape),
        vmem(BF16, *features.shape),
        vmem(BF16, *bank.shape),
        *chunked(CHUNKS, rows=PART),
        *chunked(rows=ROWS),
        vmem(BF16, CHUNKS, NX, NY, NZ, PART, channels),
        vmem(F32, ROWS, channels),
        vmem(F32, CHUNKS, NY, HALF, channels),
        *chunked(CHUNKS, rows=PART)[:6],
        vmem(F32, CHUNKS, NY, NZ, PART, channels),
        vmem(BF16, CHUNKS, NG - 1, PART, channels),
        vmem(F32, NY * HALF, channels),
        vmem(F32, NY * HALF, 128),
        vmem(F32, NY * HALF, 128),
        vmem(F32, NX, 8, 128),
        vmem(F32, NX - 1, 8, 128),
        vmem(F32, NG, 8, 128),
        vmem(F32, NX * ND, 8, 128),
        vmem(jnp.int32, queries_dp, 1),
        pltpu.SemaphoreType.DMA((N_SEMS,)),
        pltpu.SemaphoreType.DMA((4,)),
        pltpu.SemaphoreType.REGULAR((6,)),
    ]
    near, far = pl.BlockSpec(memory_space=pltpu.VMEM), pl.BlockSpec(memory_space=pl.ANY)
    loss, grad, mean = pl.pallas_call(
        lambda *refs: kernel(count_all, *refs),
        out_shape=(
            pltpu.VMEM((1, ROWS), F32),
            pltpu.VMEM((ROWS, channels), F32),
            pltpu.VMEM((1, 128), F32),
        ),
        in_specs=[far] * 4,
        out_specs=[near] * 3,
        scratch_shapes=scratch,
        compiler_params=pltpu.CompilerParams(
            collective_id=0, has_side_effects=True, vmem_limit_bytes=56 << 20
        ),
        name="patch_nce",
    )(patch_index, positions, features, bank)
    return (loss.reshape(ROWS), grad, mean[0, 0])


def solution(mesh):
    in_specs = (P("dp", "bank", None), P("dp", None), P("dp"), P("bank", None))
    out_specs = (P(("dp", "bank")), P(("dp", "bank"), None), P())
    return jax.shard_map(
        on_device, mesh=mesh, in_specs=in_specs, out_specs=out_specs, check_vma=False
    )
```

```python
import itertools
import math

import jax
import jax.numpy as jnp
from jax import lax
from jax.experimental import pallas as pl
from jax.experimental.pallas import tpu as pltpu
from jax.sharding import PartitionSpec as P

SOFTMAX_TEMP = 0.07
EPSILON = 1e-05
MESH = pl.DeviceIdType.MESH
F32, BF16 = jnp.float32, jnp.bfloat16

NY, NX, NZ, ND = 2, 4, 8, 4
NG = NY * NZ
ROWS = 32
CHUNKS = 2
PART = ROWS // CHUNKS
HALF = NZ * PART
N_SEMS = 48


def bank_id(y, x, z):
    return (y * NX + x) * NZ + z


def kernel(
    count_all,
    patch_hbm,
    pos_hbm,
    feat_hbm,
    bank_hbm,
    loss_ref,
    grad_ref,
    mean_ref,
    patch_ref, pos_ref, feat_ref, bank_ref,
    fb, fa, fu, fm, fc, fs, fz,
    pb, pa, pu, pm, pc, ps, pz,
    qa, raw,
    wf, wb, wa, wu, wm, wc, ws, wo, wz,
    acc, tacc, held,
    ts, tx, tg, ms,
    col,
    sems, lsem, heard,
):
    loads = [
        pltpu.make_async_copy(far, near, lsem.at[i])
        for i, (far, near) in enumerate(
            [(patch_hbm, patch_ref), (feat_hbm, feat_ref), (pos_hbm, pos_ref), (bank_hbm, bank_ref)]
        )
    ]
    for load in loads:
        load.start()
    place, dp = lax.axis_index("bank"), lax.axis_index("dp")
    y, x, z = place // (NX * NZ), (place // NZ) % NX, place % NZ
    xp, xo, xm = (x + 1) % NX, (x + 2) % NX, (x + 3) % NX
    x_peers = [{"bank": bank_id(y, (x + k) % NX, z)} for k in range(1, NX)]
    plus, minus = x_peers[0], x_peers[2]
    here = y * NZ + z
    g_at = [((here + k) % NG // NZ, (here + k) % NZ) for k in range(1, NG)]
    g_peers = [{"bank": bank_id(gy, x, gz)} for gy, gz in g_at]
    spot = x * ND + dp
    m_peers = []
    for k in range(1, NX * ND):
        other = (spot + k) % (NX * ND)
        m_peers.append({"dp": other % ND, "bank": bank_id(y, other // ND, z)})
    count = itertools.count()
    sent = []

    def channel():
        return sems.at[next(count)]

    def remote(src, dst, peer, out, into):
        return pltpu.make_async_remote_copy(
            src_ref=src,
            dst_ref=dst,
            send_sem=out,
            recv_sem=into,
            device_id=peer,
            device_id_type=MESH,
        )

    def take_all(sized, sem):
        pltpu.make_async_copy(sized, sized, sem).wait()

    def go(*copies):
        for copy in copies:
            copy.start()

    barrier = pltpu.get_barrier_semaphore()
    z_next = [{"bank": bank_id(y, x, (z + k) % NZ)} for k in (1, NZ - 1)]
    x_next = [plus, minus]
    greeted = x_next + z_next + [{"bank": bank_id(1 - y, x, z)}]
    greeted += [{"dp": (dp + k) % ND, "bank": place} for k in range(1, ND)]
    for peer in greeted:
        pl.semaphore_signal(barrier, inc=1, device_id=peer, device_id_type=MESH)

    def tell(i, peers):
        for peer in peers:
            pl.semaphore_signal(heard.at[i], inc=1, device_id=peer, device_id_type=MESH)

    def hear(i):
        pl.semaphore_wait(heard.at[i], 2)


    images, spots, channels = feat_ref.shape
    patches = patch_ref.shape[1]
    loads[0].wait()
    columns = jnp.transpose(patch_ref[...] - place * spots)
    loads[1].wait()
    for i in range(images):
        hit = columns[:, i : i + 1] == lax.broadcasted_iota(jnp.int32, (patches, spots), 1)
        picked = jnp.dot(hit.astype(BF16), feat_ref[i], preferred_element_type=F32).astype(BF16)
        picked = picked.reshape(patches // ROWS, CHUNKS, PART, channels)
        first = i * patches
        at = first // (NZ * ROWS)
        row = first % (NZ * ROWS) // CHUNKS
        for c in range(CHUNKS):
            fb[c, at % NX, at // NX, pl.ds(row, patches // CHUNKS), :] = picked[:, c].reshape(
                patches // CHUNKS, channels
            )
    pl.semaphore_wait(barrier, len(greeted))

    def over_x(b, a, u, m, c):
        out, across, last = channel(), channel(), channel()
        sent.append((b.at[pl.ds(0, 3)], out))
        return (
            [
                remote(b.at[xo, 0], a.at[0], plus, out, across),
                remote(b.at[xo, 1], a.at[1], minus, out, across),
            ],
            [
                remote(b.at[xp, 1], u.at[1], plus, out, last),
                remote(b.at[xm, 0], u.at[0], minus, out, last),
            ],
            [
                remote(m.at[0], c.at[0], plus, out, last),
                remote(m.at[1], c.at[1], minus, out, last),
            ],
            (a, across),
            (b.at[pl.ds(0, 2)], last),
        )

    def merge(b, a, m, copies):
        take_all(*copies[3])
        m[0] = a[0] + b[xp, 0]
        m[1] = a[1] + b[xm, 1]
        go(*copies[2])

    def x_total(b, u, c, s, copies):
        take_all(*copies[4])
        for h in range(NY):
            s[h] = (b[x, h] + u[h] + c[h]).reshape(s.shape[1:])

    def over_group(s, r):
        out, into = channel(), channel()
        sent.append((r, out))
        copies = [
            remote(s.at[gy, gz], r.at[k], peer, out, into)
            for k, ((gy, gz), peer) in enumerate(zip(g_at, g_peers))
        ]
        return copies, (r, into)

    def g_total(s, r, stage):
        take_all(*stage[1])
        total = s[y, z]
        for k in range(NG - 1):
            total = total + r[k]
        return total

    bank_dev = bank_ref.shape[0]
    wide = 2048

    def take(at, h):
        first = pl.multiple_of((h * NX + at) * NZ * ROWS, NZ * ROWS)
        rows = col[pl.ds(first, NZ * ROWS), :]
        acc[...] = jnp.zeros_like(acc)

        def some(j, _):
            start = pl.multiple_of(j * wide, wide)
            keys = lax.broadcasted_iota(jnp.int32, (NZ * ROWS, wide), 1) + start
            one = jnp.where(rows == keys, 1.0, 0.0).astype(BF16)
            acc[...] = acc[...] + jnp.dot(
                one, bank_ref[pl.ds(start, wide), :], preferred_element_type=F32
            )
            return 0

        lax.fori_loop(0, bank_dev // wide, some, 0)
        pb[at, h] = acc[...].astype(BF16)

    f = [over_x(fb.at[c], fa.at[c], fu.at[c], fm.at[c], fc.at[c]) for c in range(CHUNKS)]
    fg = [over_group(fs.at[c], fz.at[c]) for c in range(CHUNKS)]
    go(*f[0][0], *f[1][0], *f[0][1])
    tell(0, z_next)
    tell(4, x_next)
    loads[2].wait()
    columns = jnp.transpose(pos_ref[...] - place * bank_dev)
    for g in range(pos_ref.shape[0]):
        col[pl.ds(g * 128, 128), :] = columns[:, g : g + 1]
    loads[3].wait()
    p = over_x(pb, pa, pu, pm, pc)
    pg = over_group(ps, pz)
    take(xo, 0)
    hear(0)
    tell(1, z_next)
    hear(4)
    tell(5, x_next)
    take(xo, 1)
    hear(1)
    tell(2, z_next)
    merge(fb.at[0], fa.at[0], fm.at[0], f[0])
    take(xp, 1)
    hear(2)
    tell(3, z_next)
    merge(fb.at[1], fa.at[1], fm.at[1], f[1])
    go(*f[1][1])
    take(xm, 0)
    hear(3)
    hear(5)
    x_total(fb.at[0], fu.at[0], fc.at[0], fs.at[0], f[0])
    go(*fg[0][0])
    take(xp, 0)
    take(xm, 1)
    x_total(fb.at[1], fu.at[1], fc.at[1], fs.at[1], f[1])
    go(*fg[1][0])
    go(*p[0], *p[1])
    take(x, 0)
    take(x, 1)

    def unit_rows(own):
        scale = lax.rsqrt(jnp.mean(own * own, axis=-1, keepdims=True) + EPSILON)
        return own * scale / math.sqrt(channels)

    near_peers = [{"bank": bank_id(y, x, (z + k) % NZ)} for k in range(1, NZ)]
    far_peers = [{"bank": bank_id(1 - y, x, (z + k) % NZ)} for k in range(NZ)]

    def spread(c):
        out, near, far, one, two, relayed = (channel() for _ in range(6))
        sent.append((fz.at[c], out))
        more = channel()
        sent.append((fb.at[c, pl.ds(0, 3)], more))
        own = qa.at[c, x, y, z]
        mine, other = qa.at[c, x, y], qa.at[c, x, 1 - y]

        def forward(h):
            source = qa.at[c, (x + 3 + 2 * h) % NX, h]
            target = {"bank": bank_id(y, (x + 1 + 2 * h) % NX, z)}
            return remote(source, source, target, more, relayed)

        return {
            "z": [remote(own, own, peer, out, near) for peer in near_peers]
            + [remote(own, own, peer, out, far) for peer in far_peers],
            "z_in": (fz.at[c, pl.ds(0, NZ - 1)], near),
            "y_in": (fz.at[c, pl.ds(0, NZ)], far),
            "one": [remote(mine, mine, peer, more, one) for peer in (plus, minus)],
            "one_in": (fb.at[c, 0], one),
            "two": [remote(other, other, peer, more, two) for peer in (plus, minus)],
            "two_in": (fb.at[c, 0], two),
            "first": [forward(y)],
            "second": [forward(1 - y)],
            "relay_in": (fb.at[c, 0], relayed),
        }

    q = [spread(c) for c in range(CHUNKS)]

    def query_rows(c):
        own = g_total(fs.at[c], fz.at[c], fg[c]).astype(F32)
        raw[pl.ds(c * PART, PART), :] = own
        qa[c, x, y, z] = unit_rows(own).astype(BF16)
        go(*q[c]["z"])

    query_rows(0)
    merge(pb, pa, pm, p)
    query_rows(1)

    factor = 1.0 / (SOFTMAX_TEMP * math.log(2.0))
    block_keys = bank_dev // 2

    def half(query, j):
        keys = bank_ref[pl.ds(j * block_keys, block_keys), :]
        dots = lax.dot_general(query, keys, (((1,), (1,)), ((), ())), preferred_element_type=F32)
        terms = jnp.exp2(dots * factor - factor)
        some = terms[:, :128]
        for lane in range(128, block_keys, 128):
            some = some + terms[:, lane : lane + 128]
        pushed = jnp.dot(terms.astype(BF16), keys, preferred_element_type=F32)
        if j == 0:
            tacc[...] = some
            acc[...] = pushed
        else:
            tacc[...] = tacc[...] + some
            acc[...] = acc[...] + pushed

    def finish(c, places):
        sums = jnp.sum(jnp.transpose(tacc[...]), axis=0, keepdims=True)
        for i, (at, h) in enumerate(places):
            ts[at, pl.ds(NY * c + h, 1), :] = sums[:, i * HALF : (i + 1) * HALF]

    def whole(c, at):
        return qa[c, at].reshape(NY * HALF, channels)

    def unit(c, at):
        half(whole(c, at), 0)
        half(whole(c, at), 1)
        finish(c, [(at, h) for h in range(NY)])

    def pair(c, h):
        def query():
            return jnp.concatenate(
                [qa[c, at, h].reshape(HALF, channels) for at in (xp, xm)], axis=0
            )

        half(query(), 0)
        half(query(), 1)
        finish(c, [(xp, h), (xm, h)])
        wf[c, 0, h] = acc[pl.ds(0, HALF), :]
        wf[c, 1, h] = acc[pl.ds(HALF, HALF), :]

    ts[...] = jnp.zeros_like(ts)
    w = [over_x(wb.at[c], wa.at[c], wu.at[c], wm.at[c], wc.at[c]) for c in range(CHUNKS)]
    wg = [over_group(ws.at[c], wz.at[c]) for c in range(CHUNKS)]

    def push_plus(c):
        unit(c, xp)
        wf[c, 0, 0] = acc[pl.ds(0, HALF), :]
        wb[c, xp, 1] = acc[pl.ds(HALF, HALF), :].astype(BF16)
        go(w[c][1][0])

    def push_minus(c):
        unit(c, xm)
        wf[c, 1, 1] = acc[pl.ds(HALF, HALF), :]
        wb[c, xm, 0] = acc[pl.ds(0, HALF), :].astype(BF16)

    def push_halves(c):
        wb[c, xo, 0] = acc[pl.ds(0, HALF), :].astype(BF16)
        wb[c, xo, 1] = acc[pl.ds(HALF, HALF), :].astype(BF16)
        go(*w[c][0])

    def push_merged(c):
        take_all(*w[c][3])
        for h in range(NY):
            wm[c, h] = (wa[c, h].astype(F32) + wf[c, h, h]).astype(BF16)
        go(*w[c][2])

    def push_total(c):
        take_all(*w[c][4])
        for h in range(NY):
            part = wu[c, h].astype(F32) + wc[c, h].astype(F32)
            part = wo[c, h] + part.reshape(NZ, PART, channels)
            wo[c, h] = part
            ws[c, h] = part.astype(BF16)
        go(*wg[c][0])

    take_all(*q[0]["z_in"])
    go(*q[0]["one"])
    take_all(*q[0]["y_in"])
    go(*q[0]["two"])
    unit(0, x)
    wo[0] = acc[...].reshape(wo.shape[1:])
    take_all(*q[1]["z_in"])
    go(*q[1]["one"])
    take_all(*q[1]["y_in"])
    go(*q[1]["two"])
    half(whole(1, x), 0)
    wo[1] = acc[...].reshape(wo.shape[1:])
    held[...] = tacc[...]
    take_all(*q[0]["one_in"])
    go(*q[0]["first"])
    pair(0, y)
    take_all(*q[0]["two_in"])
    go(*q[0]["second"])
    x_total(pb, pu, pc, ps, p)
    go(*pg[0])
    pair(0, 1 - y)
    wb[0, xp, 1] = wf[0, 0, 1].astype(BF16)
    wb[0, xm, 0] = wf[0, 1, 0].astype(BF16)
    take_all(*q[1]["one_in"])
    go(*q[1]["first"])
    go(*w[0][1])
    take_all(*q[1]["two_in"])
    go(*q[1]["second"])
    push_plus(1)
    take_all(*q[0]["relay_in"])
    unit(0, xo)
    push_halves(0)
    take_all(*q[1]["relay_in"])
    t1_out, t1_in = channel(), channel()
    sent.append((tx, t1_out))
    t1 = [
        remote(ts.at[(x + k) % NX], tx.at[k - 1], x_peers[k - 1], t1_out, t1_in)
        for k in range(1, NX)
    ]
    unit(1, xo)
    go(t1[1], t1[0])
    push_halves(1)
    push_minus(1)
    go(t1[2])
    push_merged(0)
    go(w[1][1][1])
    acc[...] = wo[1].reshape(acc.shape)
    tacc[...] = held[...]
    half(whole(1, x), 1)
    finish(1, [(x, h) for h in range(NY)])
    wo[1] = acc[...].reshape(wo.shape[1:])

    positive = g_total(ps, pz, pg).astype(F32)
    query = qa[:, x, y, z].reshape(ROWS, channels).astype(F32)
    matched = jnp.sum(query * positive, axis=1, keepdims=True) / SOFTMAX_TEMP

    take_all(tx, t1_in)
    total = ts[x]
    for k in range(NX - 1):
        total = total + tx[k]
    line = lax.broadcasted_iota(jnp.int32, (8, 128), 0)
    tg[here] = jnp.where(
        line == 4, jnp.broadcast_to(jnp.sum(matched, axis=0, keepdims=True), (8, 128)), total
    )
    t2_out, t2_in = channel(), channel()
    others = tg.at[pl.ds(0, NG - 1)]
    sent.append((others, t2_out))
    go(*[remote(tg.at[here], tg.at[here], peer, t2_out, t2_in) for peer in g_peers])
    push_merged(1)
    push_total(0)
    push_total(1)
    take_all(others, t2_in)
    total = tg[0]
    for k in range(1, NG):
        total = total + tg[k]
    logs = jnp.sum(jnp.log(total[: NY * CHUNKS]), axis=0, keepdims=True)
    logs = jnp.sum(logs, axis=1, keepdims=True)
    quarter = logs + NG * ROWS / SOFTMAX_TEMP - total[4:5, :1]
    ms[spot] = jnp.broadcast_to(quarter, (8, 128))
    m1_out, m1_in = channel(), channel()
    rest = ms.at[pl.ds(0, NX * ND - 1)]
    sent.append((rest, m1_out))
    go(*[remote(ms.at[spot], ms.at[spot], peer, m1_out, m1_in) for peer in m_peers])

    lane = lax.broadcasted_iota(jnp.int32, (PART, HALF), 1)
    row = lax.broadcasted_iota(jnp.int32, (PART, HALF), 0)
    parts = []
    for c in range(CHUNKS):
        sums = jnp.where(y == 0, total[NY * c : NY * c + 1], total[NY * c + 1 : NY * c + 2])
        mine = jnp.where(lane == row + z * PART, jnp.broadcast_to(sums, (PART, HALF)), 0.0)
        parts.append(jnp.sum(mine, axis=1, keepdims=True))
    exponent_sum = jnp.concatenate(parts, axis=0)
    loss = jnp.log(exponent_sum) + 1.0 / SOFTMAX_TEMP - matched
    diagonal = lax.broadcasted_iota(jnp.int32, (ROWS, ROWS), 0) == lax.broadcasted_iota(
        jnp.int32, (ROWS, ROWS), 1
    )
    loss_ref[...] = jnp.sum(
        jnp.where(diagonal, jnp.broadcast_to(loss, (ROWS, ROWS)), 0.0), axis=0, keepdims=True
    )
    own = raw[...]
    scale = lax.rsqrt(jnp.mean(own * own, axis=-1, keepdims=True) + EPSILON)
    for c in range(CHUNKS):
        take_all(*wg[c][1])
        weighted = wo[c, y, z]
        for k in range(NG - 1):
            weighted = weighted + wz[c, k].astype(F32)
        some = slice(c * PART, (c + 1) * PART)
        step = (weighted / exponent_sum[some] - positive[some]) / SOFTMAX_TEMP
        inner = jnp.mean(step * own[some], axis=-1, keepdims=True)
        s = scale[some]
        grad_ref[pl.ds(c * PART, PART), :] = (s / math.sqrt(channels)) * (
            step - own[some] * (s * s * inner)
        )
    take_all(rest, m1_in)
    losses = ms[0]
    for k in range(1, NX * ND):
        losses = losses + ms[k]
    mean_ref[...] = losses[:1] / count_all
    for sized, sem in sent:
        take_all(sized, sem)


def on_device(features, patch_index, positive_index, bank):
    images, hw_dev, channels = features.shape
    queries_dp = images * patch_index.shape[1]
    count_all = queries_dp * lax.axis_size("dp")
    positions = positive_index.reshape(-1, 128)

    def vmem(dtype, *shape):
        return pltpu.VMEM(shape, dtype)

    def chunked(*lead, rows):
        return [
            vmem(BF16, *lead, NX, NY, NZ * rows, channels),
            *[vmem(BF16, *lead, NY, NZ * rows, channels) for _ in range(4)],
            vmem(BF16, *lead, NY, NZ, rows, channels),
            vmem(BF16, *lead, NG - 1, rows, channels),
        ]

    scratch = [
        vmem(jnp.int32, *patch_index.shape),
        vmem(jnp.int32, *positions.shape),
        vmem(BF16, *features.shape),
        vmem(BF16, *bank.shape),
        *chunked(CHUNKS, rows=PART),
        *chunked(rows=ROWS),
        vmem(BF16, CHUNKS, NX, NY, NZ, PART, channels),
        vmem(F32, ROWS, channels),
        vmem(F32, CHUNKS, 2, NY, HALF, channels),
        *chunked(CHUNKS, rows=PART)[:6],
        vmem(F32, CHUNKS, NY, NZ, PART, channels),
        vmem(BF16, CHUNKS, NG - 1, PART, channels),
        vmem(F32, NY * HALF, channels),
        vmem(F32, NY * HALF, 128),
        vmem(F32, NY * HALF, 128),
        vmem(F32, NX, 8, 128),
        vmem(F32, NX - 1, 8, 128),
        vmem(F32, NG, 8, 128),
        vmem(F32, NX * ND, 8, 128),
        vmem(jnp.int32, queries_dp, 1),
        pltpu.SemaphoreType.DMA((N_SEMS,)),
        pltpu.SemaphoreType.DMA((4,)),
        pltpu.SemaphoreType.REGULAR((6,)),
    ]
    near, far = pl.BlockSpec(memory_space=pltpu.VMEM), pl.BlockSpec(memory_space=pl.ANY)
    loss, grad, mean = pl.pallas_call(
        lambda *refs: kernel(count_all, *refs),
        out_shape=(
            pltpu.VMEM((1, ROWS), F32),
            pltpu.VMEM((ROWS, channels), F32),
            pltpu.VMEM((1, 128), F32),
        ),
        in_specs=[far] * 4,
        out_specs=[near] * 3,
        scratch_shapes=scratch,
        compiler_params=pltpu.CompilerParams(
            collective_id=0, has_side_effects=True, vmem_limit_bytes=56 << 20
        ),
        name="patch_nce",
    )(patch_index, positions, features, bank)
    return (loss.reshape(ROWS), grad, mean[0, 0])


def solution(mesh):
    in_specs = (P("dp", "bank", None), P("dp", None), P("dp"), P("bank", None))
    out_specs = (P(("dp", "bank")), P(("dp", "bank"), None), P())
    return jax.shard_map(
        on_device, mesh=mesh, in_specs=in_specs, out_specs=out_specs, check_vma=False
    )
```
